32 devices in a mesh: beam: 8 (over z, y), fft: 4 (over x, core).
Axes of the slice: x: 2, y: 2, z: 4, core: 2. Of those that a mesh axis runs over, the one named last changes fastest.
Arguments:
- sky_model: bfloat16 [128, 512, 512], P('beam', 'fft'), may hold values from -6 to 6
- footprint: int32 [8, 64], replicated, may hold values from 0 to 127, as said below
- profile: float32 [8, 8, 2, 4096], P('beam'), may hold values from 0.25 to 1
- chan_block: int32 [8], P('beam'), may hold values from 0 to 7
- sub_strip: int32 [8, 128, 1], P('beam'), may hold values from 0 to 3; in each aligned block of 32 rows (0 to 31, 32 to 63, ..., all dimensions but the last counted through in order) at most 16 rows name the same one
- sub_row: int32 [8, 128], P('beam'), may hold values from 0 to 4064
- sub_col: int32 [8, 128], P('beam'), may hold values from 0 to 992
- offsets: float32 [8, 128, 2, 256], P('beam'), may hold values from 2 to 29
- sub_base: int32 [8, 128], P('beam'), may hold values from 0 to 629
- gain_table: float32 [2, 630], replicated, may hold values from -3 to 3
Outputs:
- visibilities: float32 [8, 128, 2, 256], P('beam', 'fft')
The draws below stay inside these ranges and needn't reach their ends.
Inputs may be any that keep to these rules, and one draw needn't show every extreme that they name: `footprint`: each beam's list names 64 distinct sky tiles; entry i * 8 + j is the tile at tile row i and tile column j of the beam's image. At most 8 entries of one list lie in one block of 16 consecutive tile numbers, and every list reaches that. `sub_strip`: in each aligned block of 32 subgrids of a beam, at most 16 lie in one strip; some block reaches it.
All inputs are finite; a program needn't handle non-finite values.
Results may differ from the reference program's by a relative error of at most 0.0045.
Values may be sent and summed in bfloat16 or wider, within the bound.
No kernel may reach another device: no remote copies, remote signals or barrier semaphores. Data moves between devices by JAX's collectives and lax.ppermute only.
A program may use at most 192 MiB of HBM per device.

```python
import math
import jax
import jax.numpy as jnp
import numpy as np
from jax import lax

TS = 512
FT = 8
IMG = 4096
STRIP = 1024
STRIPS = 4
SKY_ROWS = 16
SKY_TILES = 128
NCHB = 8
SG = 32
NS = 256
BASE = 630
SUB_DEV = 32
PAIR_CAP = 16
NSUB = 128
N_BEAM = 8


def draw_footprint(key, part):
    beam_total = SKY_TILES // SKY_ROWS
    key_row, key_col = jax.random.split(key)
    row_start = jax.random.randint(key_row, (beam_total,), 0, SKY_ROWS - FT + 1)
    col_start = jax.random.randint(key_col, (beam_total,), 0, beam_total - FT + 1)
    stepping = jnp.arange(FT, dtype=jnp.int32)
    row_at = row_start[:, None, None] + stepping[None, :, None]
    col_at = col_start[:, None, None] + stepping[None, None, :]
    return (col_at * SKY_ROWS + row_at).reshape(beam_total, FT * FT).astype(jnp.int32)


def plant(entries, key, least, top_value):
    longest = entries.shape.index(max(entries.shape))
    spots = []
    for shift in (0, 1):
        where = [jax.random.randint(jax.random.fold_in(key, axis), (), 0, length) for axis, length in enumerate(entries.shape)]
        where[longest] = (where[longest] + shift) % entries.shape[longest]
        spots.append(tuple(where))
    return entries.at[spots[0]].set(least).at[spots[1]].set(top_value)


def block_scale(rng, shape, pieces, smallest, largest):
    def one(dim, shards_of):
        draws = jax.random.uniform(jax.random.fold_in(jax.random.fold_in(rng, 6), dim), (shards_of,), jnp.float32, smallest / len(pieces), largest / len(pieces))
        return jnp.repeat(jnp.exp(draws), shape[dim] // shards_of).reshape((-1,) + (1,) * (len(shape) - dim - 1))

    factor_of = one(*pieces[0])
    for cut in pieces[1:]:
        factor_of = factor_of * one(*cut)
    return factor_of


def routed_block(stream_key, own, number, rows, amount, top, limit, slope):
    sequence = jax.random.permutation(stream_key, amount)
    heavy_load, common = load_shares(amount, rows * top, limit, slope, True), load_shares(amount, rows * top, limit, slope, False)
    places = jnp.arange(amount)

    def named(lengths, turn):
        used = int((lengths > 0).sum())
        fixed = max(1, used // 4)
        shifted = fixed + (places - fixed + turn * (used - fixed)) % max(1, amount - fixed)
        return jnp.zeros((amount,), jnp.int32).at[sequence[jnp.where(places < fixed, places, shifted)]].set(jnp.asarray(lengths, jnp.int32))

    lengths = jnp.where(number % 4 == 0, named(heavy_load, number // 4), named(common, number - number // 4 - 1))
    mixed = jax.random.permutation(jax.random.fold_in(own, 3), amount)
    giver, receiver = mixed[0:amount // 2 * 2:2], mixed[1:amount // 2 * 2:2]
    room = jnp.minimum(lengths[giver] - 1, limit - lengths[receiver]) // 2
    room = jnp.where((giver == sequence[0]) | (receiver == sequence[0]) | (lengths[receiver] == 0), 0, jnp.maximum(room, 0))
    shifted = jax.random.randint(jax.random.fold_in(own, 4), (amount // 2,), 0, 1 << 20) % (room + 1)
    lengths = lengths.at[giver].add(-shifted).at[receiver].add(shifted)
    items = jnp.searchsorted(jnp.cumsum(lengths), jnp.arange(rows * top), side="right").astype(jnp.int32)
    grid = items.reshape(top, rows).T
    grid = grid[jax.random.permutation(jax.random.fold_in(own, 1), rows)]
    turn = jax.random.randint(jax.random.fold_in(own, 2), (rows, 1), 0, top)
    return jnp.take_along_axis(grid, (jnp.arange(top)[None, :] + turn) % top, axis=1)


def load_shares(count, total, limit, lean, full):
    weights = [(1 << 20) // math.isqrt(rank ** lean) + 1 for rank in range(1, count + 1)]
    largest = limit if full else min(limit, max(-(-total // count), total * weights[0] // sum(weights)))
    least = 1 if total - largest >= count - 1 else 0
    counts, surplus = [largest] + [least] * (count - 1), total - largest - least * (count - 1)
    while surplus > 0:
        candidates = [i for i in range(1, count) if counts[i] < largest] or [i for i in range(1, count) if counts[i] < limit]
        mass, remaining = sum([weights[i] for i in candidates]), surplus
        for i in candidates:
            more = min(limit - counts[i], max(1, remaining * weights[i] // mass), surplus)
            counts[i] = counts[i] + more
            surplus = surplus - more
    return np.array(counts)


def gaussian(own_key, dims, scale, most, shards=(), held_as=jnp.bfloat16):
    result = jax.random.normal(own_key, dims, jnp.float32) * scale
    if len(shards) > 0:
        result = block_scale(own_key, dims, shards, -0.22, 0.18) * result
    return jnp.clip(result, min=-most, max=most).astype(held_as)


def setup_inputs(seed: int = 0) -> dict:
    key_list = jax.random.split(jax.random.key(seed), 11)
    sky_model = gaussian(key_list[0], (SKY_TILES, TS, TS), 1.0, 6.0, ((0, 8), (1, 4)))
    footprint = draw_footprint(jax.random.fold_in(key_list[10], 71), 0)
    profile = jnp.clip(jnp.exp(math.log(1.0) - 1.3862944 * jax.random.uniform(key_list[2], (N_BEAM, NCHB, 2, IMG), jnp.float32) ** block_scale(key_list[2], (N_BEAM, NCHB, 2, IMG), ((0, 8),), -0.2, 0.2)), 0.25, 1.0)
    chan_block = plant(jax.random.randint(key_list[3], (N_BEAM,), 0, NCHB), jax.random.fold_in(key_list[3], 1), 0, NCHB - 1).astype(jnp.int32)
    sub_strip_keys = jax.random.split(jax.random.fold_in(key_list[4], 1), N_BEAM * NSUB // SUB_DEV)
    sub_strip_turns = jax.random.permutation(jax.random.fold_in(key_list[4], 3), N_BEAM * NSUB // SUB_DEV)
    sub_strip = jax.vmap(lambda own, number: routed_block(jax.random.fold_in(key_list[4], 2), own, number, SUB_DEV, STRIPS, 1, PAIR_CAP, 2))(sub_strip_keys, sub_strip_turns).reshape((N_BEAM, NSUB, 1))
    sub_row = plant(jax.random.randint(key_list[5], (N_BEAM, NSUB), 0, IMG - SG + 1), jax.random.fold_in(key_list[5], 1), 0, IMG - SG).astype(jnp.int32)
    sub_col = plant(jax.random.randint(key_list[6], (N_BEAM, NSUB), 0, STRIP - SG + 1), jax.random.fold_in(key_list[6], 1), 0, STRIP - SG).astype(jnp.int32)
    offsets = jnp.clip(2.0 + 27.0 * jax.random.uniform(key_list[7], (N_BEAM, NSUB, 2, NS), jnp.float32) ** block_scale(key_list[7], (N_BEAM, NSUB, 2, NS), ((0, 8),), -0.2, 0.2), 2.0, 29.0)
    sub_base = plant(jax.random.randint(key_list[8], (N_BEAM, NSUB), 0, BASE), jax.random.fold_in(key_list[8], 1), 0, BASE - 1).astype(jnp.int32)
    gain_table = gaussian(key_list[9], (2, BASE), 0.7, 3.0, (), jnp.float32)
    return dict(sky_model=sky_model, footprint=footprint, profile=profile, chan_block=chan_block, sub_strip=sub_strip, sub_row=sub_row, sub_col=sub_col, offsets=offsets, sub_base=sub_base, gain_table=gain_table)


kernel_width = 1.5

def beam_grid(sky_model, tile_ids, chosen_prof):
    fetched = jnp.take(sky_model, tile_ids, axis=0).astype(jnp.float32)
    sky_image = fetched.reshape(FT, FT, TS, TS).transpose(0, 2, 1, 3).reshape(IMG, IMG)
    sky_image = sky_image * chosen_prof[0][:, None] * chosen_prof[1][None, :]
    norm_scale = 1.0 / math.sqrt(IMG)
    spectrum = jnp.fft.fft(sky_image, axis=1) * norm_scale
    part_re = jnp.real(spectrum).astype(jnp.bfloat16)
    part_im = jnp.imag(spectrum).astype(jnp.bfloat16)
    part_re, part_im = lax.optimization_barrier((part_re, part_im))
    spectrum = lax.complex(part_re.astype(jnp.float32), part_im.astype(jnp.float32))
    grid_full = jnp.fft.fft(spectrum, axis=0) * norm_scale
    return (jnp.real(grid_full), jnp.imag(grid_full))

def predict(cut_re, cut_im, sample_pos, base_ids, gain_table):
    places = jnp.arange(SG, dtype=jnp.float32)
    weight_u = jnp.exp(-jnp.square((places[None, None, :] - sample_pos[:, 0, :, None]) / kernel_width))
    weight_v = jnp.exp(-jnp.square((places[None, None, :] - sample_pos[:, 1, :, None]) / kernel_width))
    inner_re = jnp.einsum('bna,bac->bnc', weight_u, cut_re, precision=lax.Precision.HIGHEST)
    inner_im = jnp.einsum('bna,bac->bnc', weight_u, cut_im, precision=lax.Precision.HIGHEST)
    summed_re = lax.optimization_barrier(jnp.sum(inner_re * weight_v, axis=-1))
    summed_im = lax.optimization_barrier(jnp.sum(inner_im * weight_v, axis=-1))
    gain_re = gain_table[0][base_ids][:, None]
    gain_im = gain_table[1][base_ids][:, None]
    out_re = gain_re * summed_re - gain_im * summed_im
    out_im = gain_re * summed_im + gain_im * summed_re
    return jnp.stack([out_re, out_im], axis=1)

def reference(sky_model, footprint, profile, chan_block, sub_strip, sub_row, sub_col, offsets, sub_base, gain_table):
    results = []
    for beam_index in range(N_BEAM):
        chosen_prof = profile[beam_index, chan_block[beam_index]]
        grid_re, grid_im = beam_grid(sky_model, footprint[beam_index], chosen_prof)
        first_rows = sub_row[beam_index].astype(jnp.int32)
        first_cols = (sub_strip[beam_index, :, 0] * STRIP + sub_col[beam_index]).astype(jnp.int32)

        def cut_one(field, row_at, col_at):
            return lax.dynamic_slice(field, (row_at, col_at), (SG, SG))
        cut_re = jax.vmap(lambda row_at, col_at: cut_one(grid_re, row_at, col_at))(first_rows, first_cols)
        cut_im = jax.vmap(lambda row_at, col_at: cut_one(grid_im, row_at, col_at))(first_rows, first_cols)
        results.append(predict(cut_re, cut_im, offsets[beam_index], sub_base[beam_index], gain_table))
    return jnp.stack(results, axis=0)
```

```python
import functools
import math

import jax
import jax.numpy as jnp
import ml_dtypes
import numpy as np
from jax import lax
from jax.experimental import pallas as pl
from jax.experimental.pallas import tpu as pltpu
from jax.sharding import PartitionSpec as P

FT = 8
SG = 32
CAP = 8
LANES = 128

kernel_width = 1.5
highest = lax.Precision.HIGHEST
f32 = jnp.float32
bf16 = jnp.bfloat16


def round_up(number, unit):
    return -(-number // unit) * unit


def phase_table(rows, cols, period):
    residue = np.arange(rows)[:, None] * np.arange(cols)[None, :] % period
    angle = residue * (2.0 * math.pi / period)
    return np.cos(angle), -np.sin(angle)


def unit_phase(residue, period):
    angle = residue.astype(f32) * (2.0 * math.pi / period)
    return jnp.cos(angle), -jnp.sin(angle)


def window_kernel(
    tix_ref, r0_ref, c0_ref,
    own_ref, oth_ref, p1_ref, p0_ref, tcos_ref, tsin_ref,
    lr0_ref, li0_ref, lr1_ref, li1_ref, ar_ref, ai_ref, br_ref, bi_ref,
    g_ref, rs_ref, *, chunk,
):
    q = pl.program_id(0)
    v_rows = rs_ref.shape[2]
    chunks = v_rows // chunk

    def one_tile(k, carry):
        t = tix_ref[q, k]
        scale = p1_ref[0, pl.ds(k, 1), :]
        own = (own_ref[t].astype(f32) * scale).astype(bf16)
        oth = (oth_ref[t].astype(f32) * scale).astype(bf16)
        both = jnp.concatenate([own, oth], axis=0)
        row_scale = p0_ref[0, pl.ds(k, 1), :]

        def one_chunk(i, inner):
            at = pl.multiple_of(i * chunk, chunk)
            for c, table in enumerate((tcos_ref, tsin_ref)):
                got = lax.dot_general(
                    table[pl.ds(at, chunk), :], both, (((1,), (1,)), ((), ())),
                    preferred_element_type=f32,
                ) * row_scale
                for h in range(2):
                    rs_ref[(h * 2 + c), k, pl.ds(at, chunk), :] = got[:, h * LANES:(h + 1) * LANES]
            return inner

        return lax.fori_loop(0, chunks, one_chunk, carry)

    lax.fori_loop(0, CAP, one_tile, 0)

    lane = lax.broadcasted_iota(jnp.int32, (2 * SG, LANES), 1)
    is_low = (lane // SG) == 1

    def one_sub(s, carry):
        r0 = r0_ref[q, s]
        c0 = c0_ref[q, s]
        rows = []
        for k in range(CAP):
            rows.append(jnp.concatenate(
                [rs_ref[j, k, pl.ds(c0, SG), :].astype(bf16) for j in range(4)], axis=1))
        windows = jnp.concatenate(rows, axis=0)
        lr0 = lr0_ref[pl.ds(r0, SG), :].astype(bf16)
        li0 = li0_ref[pl.ds(r0, SG), :].astype(bf16)
        lr1 = lr1_ref[pl.ds(r0, SG), :].astype(bf16)
        li1 = li1_ref[pl.ds(r0, SG), :].astype(bf16)
        left = jnp.concatenate([
            jnp.concatenate([lr0, -li0, lr1, -li1], axis=1),
            jnp.concatenate([li0, lr0, li1, lr1], axis=1),
        ], axis=0)
        out = lax.dot_general(left, windows, (((1,), (1,)), ((), ())), preferred_element_type=f32)
        r8 = lax.rem(r0, 8)
        c8 = lax.rem(c0, 8)
        ar, ai = ar_ref[0, r8], ai_ref[0, r8]
        br, bi = br_ref[0, c8], bi_ref[0, c8]
        fr = ar * br - ai * bi
        fi = ar * bi + ai * br
        re_parts, im_parts = [], []
        for a in range(SG // 8):
            re = out[a * 8:(a + 1) * 8]
            im = out[SG + a * 8:SG + (a + 1) * 8]
            re_parts.append(re * fr - im * fi)
            im_parts.append(re * fi + im * fr)
        full = jnp.concatenate(re_parts + im_parts, axis=0)
        half = full[:, :LANES] + full[:, LANES:]
        half = half + pltpu.roll(half, 2 * SG, 1)
        half = half + pltpu.roll(half, SG, 1)
        high = half.astype(bf16)
        low = half - high.astype(f32)
        g_ref[0, s] = jnp.where(is_low, low, half).astype(bf16)
        return carry

    lax.fori_loop(0, r0_ref.shape[1], one_sub, 0)


def degrid_kernel(g_ref, off_ref, out_ref, acc_ref):
    subs = g_ref.shape[1]
    samples = off_ref.shape[3]
    places = lax.broadcasted_iota(jnp.int32, (SG, samples), 0).astype(f32)
    factor = -math.log2(math.e) / kernel_width**2
    blank = jnp.zeros((LANES - 3 * SG, samples), bf16)

    def one_sub(s, carry):
        tu = places - off_ref[0, s, 0:1, :]
        tv = places - off_ref[0, s, 1:2, :]
        wu = jnp.exp2(tu * tu * factor)
        wv = jnp.exp2(tv * tv * factor)
        wv_high = wv.astype(bf16)
        wv_low = (wv - wv_high.astype(f32)).astype(bf16)
        right = jnp.concatenate([wv_high, wv_high, wv_low, blank], axis=0)
        inner = jnp.dot(g_ref[0, s], right, preferred_element_type=f32)
        re = jnp.sum(inner[:SG] * wu, axis=0, keepdims=True)
        im = jnp.sum(inner[SG:] * wu, axis=0, keepdims=True)
        acc_ref[pl.ds(s, 1), :] = jnp.concatenate([re, im], axis=1)
        return carry

    lax.fori_loop(0, subs, one_sub, 0, unroll=4)
    out_ref[0, 0, 0] = acc_ref[...].astype(out_ref.dtype)


def local(
    sky_model, footprint, profile, chan_block, sub_strip, sub_row, sub_col,
    offsets, sub_base, gain_table,
):
    axes = ("beam", "fft")
    beams = lax.axis_size("beam")
    ffts = lax.axis_size("fft")
    my_beam = lax.axis_index("beam")
    my_fft = lax.axis_index("fft")
    my_core = my_fft % 2
    quads = beams // 2
    pairs = ffts // 2
    tiles_dev, tile_rows, tile_side = sky_model.shape
    image_side = FT * tile_side
    half_side = image_side // 2
    subs = sub_row.shape[1]
    sub_dev = subs // ffts
    samples = offsets.shape[3]
    strip_cols = image_side // ffts

    def turn(step):
        out = []
        for b in range(beams):
            for f in range(ffts):
                target = (2 * ((b // 2 - step) % quads) + f % 2) * ffts + 2 * (f // 2) + b % 2
                out.append((b * ffts + f, target))
        return out

    oth_sky = lax.ppermute(sky_model, "fft", [(f, f ^ 1) for f in range(ffts)])

    channel_pick = (jnp.arange(profile.shape[1], dtype=jnp.int32) == chan_block[0]).astype(f32)
    chosen = jnp.sum(profile[0] * channel_pick[:, None, None], axis=0)
    col_at = sub_strip[0, :, 0] * strip_cols + sub_col[0]
    mirrored = col_at >= half_side
    r0_mine = jnp.where(mirrored, (image_side - (SG - 1) - sub_row[0]) % image_side, sub_row[0])
    c0_mine = jnp.where(mirrored, image_side - (SG - 1) - col_at, col_at)
    off_mine = jnp.where(mirrored[:, None, None], (SG - 1) - offsets[0], offsets[0])
    small = jnp.concatenate([chosen.reshape(-1), r0_mine.astype(f32), c0_mine.astype(f32)]).reshape(-1, LANES)
    steps = [(my_beam // 2 + t) % quads for t in range(quads)]
    smalls = jnp.stack([lax.ppermute(small, axes, turn(t)) for t in range(quads)]).reshape(quads, -1)
    offs = jnp.stack([lax.ppermute(off_mine, axes, turn(t)) for t in range(quads)])
    beam_ids = jnp.stack([2 * s + my_core for s in steps])
    prof = smalls[:, :2 * image_side].reshape(quads, 2, image_side)
    r0_all = smalls[:, 2 * image_side:2 * image_side + subs].astype(jnp.int32)
    c0_all = smalls[:, 2 * image_side + subs:].astype(jnp.int32)

    lists = jnp.take(footprint, beam_ids, axis=0)
    hits = (lists // tiles_dev == my_beam).astype(jnp.int32)
    order = jnp.cumsum(hits, axis=1) - 1
    slots = hits[:, :, None] * (order[:, :, None] == jnp.arange(CAP, dtype=jnp.int32)[None, None, :])
    tix = jnp.sum(slots * (lists % tiles_dev)[:, :, None], axis=1)
    place = jnp.sum(slots * jnp.arange(FT * FT, dtype=jnp.int32)[None, :, None], axis=1)
    valid = jnp.sum(slots, axis=1).astype(f32)
    tile_i, tile_j = place // FT, place % FT
    eights = jnp.arange(FT, dtype=jnp.int32)
    pick_i = (tile_i[:, :, None] == eights).astype(f32) * valid[:, :, None]
    pick_j = (tile_j[:, :, None] == eights).astype(f32)
    prof_u = prof[:, 0].reshape(quads, FT, ffts, tile_rows)
    fft_ids = jnp.stack([my_fft, my_fft + 1 - 2 * my_core])
    prof_u = jnp.take(prof_u, fft_ids, axis=2)
    prof_u = jnp.pad(prof_u, ((0, 0), (0, 0), (0, 0), (0, LANES - tile_rows))).reshape(quads, FT, 2 * LANES)
    p0 = jnp.sum(pick_i[:, :, :, None] * prof_u[:, None], axis=2)
    p1 = jnp.sum(pick_j[:, :, :, None] * prof[:, 1].reshape(quads, 1, FT, tile_side), axis=2)

    lane_e = jnp.arange(CAP * SG, dtype=jnp.int32) % SG
    lane_i = jnp.repeat(tile_i, SG, axis=1)
    lane_j = jnp.repeat(tile_j, SG, axis=1)
    ar, ai = unit_phase(
        lane_i[:, None, None, :] * (eights[:, None] + eights[None, :])[None, :, :, None] % FT, FT)
    br, bi = unit_phase(
        lane_j[:, None, :] * (eights[None, :, None] + lane_e[None, None, :]) % FT, FT)
    br = jnp.broadcast_to(br[:, :, None, :], ar.shape)
    bi = jnp.broadcast_to(bi[:, :, None, :], ai.shape)

    chunk = 344
    v_rows = 6 * chunk
    t_cos, t_sin = phase_table(v_rows, tile_side, image_side)
    t_cos, t_sin = jnp.asarray(t_cos.astype(ml_dtypes.bfloat16)), jnp.asarray(t_sin.astype(ml_dtypes.bfloat16))
    u_rows = image_side + SG
    u_cos, u_sin = phase_table(u_rows, LANES, image_side)
    u_cos, u_sin = jnp.asarray(u_cos.astype(np.float32)), jnp.asarray(u_sin.astype(np.float32))
    shift_r, shift_i = unit_phase(
        fft_ids[:, None] * tile_rows * jnp.arange(u_rows, dtype=jnp.int32)[None, :] % image_side, image_side)
    left = []
    for h in range(2):
        sr, si = shift_r[h][:, None], shift_i[h][:, None]
        left += [u_cos * sr - u_sin * si, u_cos * si + u_sin * sr]

    pad_rows = ((0, 0), (0, LANES - tile_rows), (0, 0))
    own_sky, oth_sky = (jnp.pad(s, pad_rows) if tile_rows < LANES else s for s in (sky_model, oth_sky))

    whole = lambda a: pl.BlockSpec(a.shape, lambda q, *_: (0,) * a.ndim, pipeline_mode=pl.Buffered(1))
    per_beam = lambda a: pl.BlockSpec((1,) + a.shape[1:], lambda q, *_: (q,) + (0,) * (a.ndim - 1))
    fixed = [own_sky, oth_sky]
    operands = (own_sky, oth_sky, p1, p0, t_cos, t_sin, *left, ar, ai, br, bi)
    specs = [whole(own_sky), whole(oth_sky), per_beam(p1), per_beam(p0), whole(t_cos), whole(t_sin)]
    specs += [whole(x) for x in left] + [per_beam(x) for x in (ar, ai, br, bi)]
    cuts = pl.pallas_call(
        functools.partial(window_kernel, chunk=chunk),
        out_shape=jax.ShapeDtypeStruct((quads, subs, 2 * SG, LANES), bf16),
        grid_spec=pltpu.PrefetchScalarGridSpec(
            num_scalar_prefetch=3, grid=(quads,), in_specs=specs,
            out_specs=pl.BlockSpec((1, subs, 2 * SG, LANES), lambda q, *_: (q, 0, 0, 0)),
            scratch_shapes=[pltpu.VMEM((4, CAP, v_rows, LANES), f32)],
        ),
        compiler_params=pltpu.CompilerParams(vmem_limit_bytes=63 << 20),
        name="windows",
    )(tix, r0_all, c0_all, *operands)

    partial = pl.pallas_call(
        degrid_kernel,
        grid=(quads, ffts),
        in_specs=[
            pl.BlockSpec((1, sub_dev, 2 * SG, LANES), lambda q, f: (q, f, 0, 0)),
            pl.BlockSpec((1, sub_dev, 2, samples), lambda q, f: (q, f, 0, 0)),
        ],
        out_specs=pl.BlockSpec((1, 1, 1, sub_dev, 2 * samples), lambda q, f: (q, f % 2, f // 2, 0, 0)),
        out_shape=jax.ShapeDtypeStruct((quads, 2, pairs, sub_dev, 2 * samples), bf16),
        scratch_shapes=[pltpu.VMEM((sub_dev, 2 * samples), f32)],
        compiler_params=pltpu.CompilerParams(vmem_limit_bytes=32 << 20),
        name="degrid",
    )(cuts, offs)

    partial = jnp.roll(partial, my_beam // 2, axis=0)
    groups = [[b * ffts + 2 * x + c for b in range(beams) for x in range(pairs)] for c in range(2)]
    parts = partial.reshape(beams * pairs, sub_dev, 2 * samples)
    came = lax.all_to_all(parts, axes, 0, 0, tiled=True, axis_index_groups=groups)
    total = jnp.sum(came.astype(f32), axis=0)
    total = lax.ppermute(total, axes, turn(0)) * (1.0 / image_side)
    total = total.reshape(sub_dev, 2, samples)

    mine = lambda a: lax.dynamic_slice_in_dim(a, my_fft * sub_dev, sub_dev, 0)
    base_hot = (mine(sub_base[0])[:, None] == jnp.arange(gain_table.shape[1], dtype=jnp.int32)[None, :]).astype(f32)
    gains = jnp.dot(base_hot, gain_table.T, precision=highest)
    g0, g1 = gains[:, 0:1], gains[:, 1:2]
    re = total[:, 0]
    im = jnp.where(mine(mirrored)[:, None], -total[:, 1], total[:, 1])
    return jnp.stack([g0 * re - g1 * im, g0 * im + g1 * re], axis=1)[None]


def solution(mesh):
    return jax.shard_map(
        local,
        mesh=mesh,
        in_specs=(
            P("beam", "fft", None), P(), P("beam", None, None, None), P("beam"),
            P("beam", None, None), P("beam", None), P("beam", None),
            P("beam", None, None, None), P("beam", None), P(),
        ),
        out_specs=P("beam", "fft", None, None),
        check_vma=False,
    )
```

```python
import functools
import math

import jax
import jax.numpy as jnp
from jax import lax
from jax.experimental import pallas as pl
from jax.experimental.pallas import tpu as pltpu
from jax.sharding import PartitionSpec as P

FT = 8
SG = 32
CAP = 8
LANES = 128

kernel_width = 1.5
highest = lax.Precision.HIGHEST
f32 = jnp.float32
bf16 = jnp.bfloat16


def round_up(number, unit):
    return -(-number // unit) * unit


def unit_phase(residue, period):
    angle = residue.astype(f32) * (2.0 * math.pi / period)
    return jnp.cos(angle), -jnp.sin(angle)


def split_phase(coarse, fine, width, step, offset, period):
    col = step * jnp.arange(width, dtype=jnp.int32) + offset
    cr, ci = unit_phase(fine * jnp.arange(coarse, dtype=jnp.int32)[:, None] * col % period, period)
    fr, fi = unit_phase(jnp.arange(fine, dtype=jnp.int32)[:, None] * col % period, period)
    cr, ci, fr, fi = cr[:, None], ci[:, None], fr[None], fi[None]
    return (
        (cr * fr - ci * fi).reshape(coarse * fine, width),
        (cr * fi + ci * fr).reshape(coarse * fine, width),
    )


def window_kernel(
    tix_ref, r0_ref, c0_ref, wr_ref, wi_ref,
    own_hi_ref, own_lo_ref, oth_hi_ref, oth_lo_ref, p1_hi_ref, p1_lo_ref, p0_ref,
    tcos_ref, tsin_ref, lr0_ref, li0_ref, lr1_ref, li1_ref,
    ar_ref, ai_ref, br_ref, bi_ref,
    g_ref, rs_ref, *, unroll,
):
    q = pl.program_id(0)

    def one_tile(k, carry):
        t = tix_ref[q, k]
        scale_hi = p1_hi_ref[0, pl.ds(k, 1), :]
        scale_lo = p1_lo_ref[0, pl.ds(k, 1), :]
        even, odd = [], []
        for hi_ref, lo_ref in ((own_hi_ref, own_lo_ref), (oth_hi_ref, oth_lo_ref)):
            hi = hi_ref[t].astype(f32) * scale_hi
            lo = lo_ref[t].astype(f32) * scale_lo
            even.append((hi + lo).astype(bf16))
            odd.append((hi - lo).astype(bf16))
        row_scale = p0_ref[0, pl.ds(k, 1), :]
        for c, (table, halves) in enumerate(((tcos_ref, even), (tsin_ref, odd))):
            got = lax.dot_general(
                table[...], jnp.concatenate(halves, axis=0), (((1,), (1,)), ((), ())),
                preferred_element_type=f32,
            ) * row_scale
            for h in range(2):
                rs_ref[h * 2 + c, k] = got[:, h * LANES:(h + 1) * LANES]
        return carry

    lax.fori_loop(0, CAP, one_tile, 0)

    lane = lax.broadcasted_iota(jnp.int32, (2 * SG, LANES), 1)
    is_low = (lane // SG) == 1

    def one_sub(s):
        r0 = r0_ref[q, s]
        c0 = c0_ref[q, s]
        windows = jnp.concatenate([
            jnp.concatenate([rs_ref[j, k, pl.ds(c0, SG), :].astype(bf16) for j in range(4)], axis=1)
            for k in range(CAP)
        ], axis=0)
        lr0, li0, lr1, li1 = (
            ref[pl.ds(r0, SG), :].astype(bf16) for ref in (lr0_ref, li0_ref, lr1_ref, li1_ref))
        left = jnp.concatenate([
            jnp.concatenate([lr0, -li0, lr1, -li1], axis=1),
            jnp.concatenate([li0, lr0, li1, lr1], axis=1),
        ], axis=0)
        out = lax.dot_general(left, windows, (((1,), (1,)), ((), ())), preferred_element_type=f32)
        r8, c8 = lax.rem(r0, 8), lax.rem(c0, 8)
        ar, ai = ar_ref[0, r8], ai_ref[0, r8]
        br, bi = br_ref[0, c8], bi_ref[0, c8]
        wr, wi = wr_ref[q, s], wi_ref[q, s]
        br, bi = br * wr - bi * wi, br * wi + bi * wr
        fr = ar * br - ai * bi
        fi = ar * bi + ai * br
        re_parts, im_parts = [], []
        for a in range(SG // 8):
            re = out[a * 8:(a + 1) * 8]
            im = out[SG + a * 8:SG + (a + 1) * 8]
            re_parts.append(re * fr - im * fi)
            im_parts.append(re * fi + im * fr)
        full = jnp.concatenate(re_parts + im_parts, axis=0)
        half = full[:, :LANES] + full[:, LANES:]
        half = half + pltpu.roll(half, 2 * SG, 1)
        half = half + pltpu.roll(half, SG, 1)
        high = half.astype(bf16)
        low = half - high.astype(f32)
        g_ref[0, s] = jnp.where(is_low, low, half).astype(bf16)

    def some_subs(i, carry):
        for u in range(unroll):
            one_sub(i * unroll + u)
        return carry

    lax.fori_loop(0, r0_ref.shape[1] // unroll, some_subs, 0)


def degrid_kernel(turn_ref, g_ref, off_ref, out_ref, acc_ref, *, unroll):
    subs = g_ref.shape[1]
    samples = off_ref.shape[3]
    places = lax.broadcasted_iota(jnp.int32, (SG, samples), 0).astype(f32)
    factor = -math.log2(math.e) / kernel_width**2
    blank = jnp.zeros((LANES - 3 * SG, samples), bf16)

    def one_sub(s):
        tu = places - off_ref[0, s, 0:1, :]
        tv = places - off_ref[0, s, 1:2, :]
        wu = jnp.exp2(tu * tu * factor)
        wv = jnp.exp2(tv * tv * factor)
        wv_high = wv.astype(bf16)
        wv_low = (wv - wv_high.astype(f32)).astype(bf16)
        right = jnp.concatenate([wv_high, wv_high, wv_low, blank], axis=0)
        inner = jnp.dot(g_ref[0, s], right, preferred_element_type=f32)
        re = jnp.sum(inner[:SG] * wu, axis=0, keepdims=True)
        im = jnp.sum(inner[SG:] * wu, axis=0, keepdims=True)
        acc_ref[pl.ds(s, 1), :] = jnp.concatenate([re, im], axis=1)

    def some_subs(i, carry):
        for u in range(unroll):
            one_sub(i * unroll + u)
        return carry

    lax.fori_loop(0, subs // unroll, some_subs, 0)
    out_ref[0, 0, 0] = acc_ref[...].astype(out_ref.dtype)


def local(
    sky_model, footprint, profile, chan_block, sub_strip, sub_row, sub_col,
    offsets, sub_base, gain_table,
):
    axes = ("beam", "fft")
    beams = lax.axis_size("beam")
    ffts = lax.axis_size("fft")
    my_beam = lax.axis_index("beam")
    my_fft = lax.axis_index("fft")
    my_core = my_fft % 2
    quads = beams // 2
    pairs = ffts // 2
    tiles_dev, tile_rows, tile_side = sky_model.shape
    image_side = FT * tile_side
    half_side = image_side // 2
    subs = sub_row.shape[1]
    sub_dev = subs // ffts
    samples = offsets.shape[3]
    strip_cols = image_side // ffts

    def turn(step):
        out = []
        for b in range(beams):
            for f in range(ffts):
                target = (2 * ((b // 2 - step) % quads) + f % 2) * ffts + 2 * (f // 2) + b % 2
                out.append((b * ffts + f, target))
        return out

    oth_sky = lax.ppermute(sky_model, "fft", [(f, f ^ 1) for f in range(ffts)])

    channel_pick = (jnp.arange(profile.shape[1], dtype=jnp.int32) == chan_block[0]).astype(f32)
    chosen = jnp.sum(profile[0] * channel_pick[:, None, None], axis=0)
    col_at = sub_strip[0, :, 0] * strip_cols + sub_col[0]
    mirrored = col_at >= half_side
    r0_mine = jnp.where(mirrored, (image_side - (SG - 1) - sub_row[0]) % image_side, sub_row[0])
    c0_mine = jnp.where(mirrored, image_side - (SG - 1) - col_at, col_at)
    off_mine = jnp.where(mirrored[:, None, None], (SG - 1) - offsets[0], offsets[0])
    small = jnp.concatenate([chosen.reshape(-1), r0_mine.astype(f32), c0_mine.astype(f32)]).reshape(-1, LANES)
    steps = [(my_beam // 2 + t) % quads for t in range(quads)]
    smalls = jnp.stack([lax.ppermute(small, axes, turn(t)) for t in range(quads)]).reshape(quads, -1)
    smalls, off_mine = lax.optimization_barrier((smalls, off_mine))
    offs = [lax.ppermute(off_mine, axes, turn(t)) for t in range(quads)]
    beam_ids = jnp.stack([2 * s + my_core for s in steps])
    prof = smalls[:, :2 * image_side].reshape(quads, 2, image_side)
    r0_all = smalls[:, 2 * image_side:2 * image_side + subs].astype(jnp.int32)
    c0_all = smalls[:, 2 * image_side + subs:].astype(jnp.int32)

    lists = jnp.take(footprint, beam_ids, axis=0)
    hits = (lists // tiles_dev == my_beam).astype(jnp.int32)
    order = jnp.cumsum(hits, axis=1) - 1
    slots = hits[:, :, None] * (order[:, :, None] == jnp.arange(CAP, dtype=jnp.int32)[None, None, :])
    tix = jnp.sum(slots * (lists % tiles_dev)[:, :, None], axis=1)
    place = jnp.sum(slots * jnp.arange(FT * FT, dtype=jnp.int32)[None, :, None], axis=1)
    valid = jnp.sum(slots, axis=1).astype(f32)
    tile_i, tile_j = place // FT, place % FT
    eights = jnp.arange(FT, dtype=jnp.int32)
    pick_i = (tile_i[:, :, None] == eights).astype(f32) * valid[:, :, None]
    pick_j = (tile_j[:, :, None] == eights).astype(f32)
    prof_u = prof[:, 0].reshape(quads, FT, ffts, tile_rows)
    fft_ids = jnp.stack([my_fft, my_fft + 1 - 2 * my_core])
    prof_u = jnp.take(prof_u, fft_ids, axis=2)
    prof_u = jnp.pad(prof_u, ((0, 0), (0, 0), (0, 0), (0, LANES - tile_rows))).reshape(quads, FT, 2 * LANES)
    p0 = jnp.sum(pick_i[:, :, :, None] * prof_u[:, None], axis=2)
    p1 = jnp.sum(pick_j[:, :, :, None] * prof[:, 1].reshape(quads, 1, FT, tile_side), axis=2)

    lane_e = jnp.arange(CAP * SG, dtype=jnp.int32) % SG
    lane_i = jnp.repeat(tile_i, SG, axis=1)
    lane_j = jnp.repeat(tile_j, SG, axis=1)
    ar, ai = unit_phase(
        lane_i[:, None, None, :] * (eights[:, None] + eights[None, :])[None, :, :, None] % FT, FT)
    middle = 2 * image_side
    br, bi = unit_phase(
        (middle // FT * lane_j[:, None, :] * (eights[None, :, None] + lane_e[None, None, :])
         + (tile_side - 1) * lane_e[None, None, :]) % middle, middle)
    wr, wi = unit_phase((tile_side - 1) * c0_all % middle, middle)
    br = jnp.broadcast_to(br[:, :, None, :], ar.shape)
    bi = jnp.broadcast_to(bi[:, :, None, :], ai.shape)

    side_half = tile_side // 2
    t_cos, t_sin = split_phase(129, 16, side_half, 2, 1, 2 * image_side)
    t_cos, t_sin = t_cos.astype(bf16), t_sin.astype(bf16)
    v_rows = t_cos.shape[0]
    left = []
    for h in range(2):
        coarse, fine = (image_side + SG) // SG, SG
        col = fft_ids[h] * tile_rows + jnp.arange(LANES, dtype=jnp.int32)
        cr, ci = unit_phase(fine * jnp.arange(coarse, dtype=jnp.int32)[:, None] * col % image_side, image_side)
        fr, fi = unit_phase(jnp.arange(fine, dtype=jnp.int32)[:, None] * col % image_side, image_side)
        cr, ci, fr, fi = cr[:, None], ci[:, None], fr[None], fi[None]
        left += [(cr * fr - ci * fi).reshape(-1, LANES), (cr * fi + ci * fr).reshape(-1, LANES)]

    flip = jnp.arange(side_half)[:, None] + jnp.arange(side_half)[None, :] == side_half - 1
    halves = []
    for sky in (sky_model, oth_sky):
        if tile_rows < LANES:
            sky = jnp.pad(sky, ((0, 0), (0, LANES - tile_rows), (0, 0)))
        low = jnp.einsum("trx,xy->try", sky[:, :, :side_half], flip.astype(bf16), preferred_element_type=f32)
        halves += [sky[:, :, side_half:], low.astype(bf16)]
    p1_lo = jnp.flip(p1[:, :, :side_half], axis=2)
    p1_hi = p1[:, :, side_half:]

    whole = lambda a: pl.BlockSpec(a.shape, lambda q, *_: (0,) * a.ndim, pipeline_mode=pl.Buffered(1))
    per_beam = lambda a: pl.BlockSpec((1,) + a.shape[1:], lambda q, *_: (q,) + (0,) * (a.ndim - 1))
    tables = [t_cos, t_sin, *left]
    slabs, phases = [p1_hi, p1_lo, p0], [ar, ai, br, bi]
    operands = halves + slabs + tables + phases
    specs = [whole(x) for x in halves] + [per_beam(x) for x in slabs]
    specs += [whole(x) for x in tables] + [per_beam(x) for x in phases]
    cuts = pl.pallas_call(
        functools.partial(window_kernel, unroll=16),
        out_shape=jax.ShapeDtypeStruct((quads, subs, 2 * SG, LANES), bf16),
        grid_spec=pltpu.PrefetchScalarGridSpec(
            num_scalar_prefetch=5, grid=(quads,), in_specs=specs,
            out_specs=pl.BlockSpec((1, subs, 2 * SG, LANES), lambda q, *_: (q, 0, 0, 0)),
            scratch_shapes=[pltpu.VMEM((4, CAP, v_rows, LANES), f32)],
        ),
        compiler_params=pltpu.CompilerParams(vmem_limit_bytes=63 << 20),
        name="windows",
    )(tix, r0_all, c0_all, wr, wi, *operands)

    offs, cuts = lax.optimization_barrier((offs, cuts))
    offs = jnp.stack(offs)
    home = (my_beam // 2).astype(jnp.int32).reshape(1)
    partial = pl.pallas_call(
        functools.partial(degrid_kernel, unroll=8),
        grid_spec=pltpu.PrefetchScalarGridSpec(
            num_scalar_prefetch=1, grid=(quads, ffts),
            in_specs=[
                pl.BlockSpec((1, sub_dev, 2 * SG, LANES), lambda q, f, _: (q, f, 0, 0)),
                pl.BlockSpec((1, sub_dev, 2, samples), lambda q, f, _: (q, f, 0, 0)),
            ],
            out_specs=pl.BlockSpec(
                (1, 1, 1, sub_dev, 2 * samples),
                lambda q, f, home: (lax.rem(q + home[0], quads), lax.rem(f, 2), f // 2, 0, 0)),
            scratch_shapes=[pltpu.VMEM((sub_dev, 2 * samples), f32)],
        ),
        out_shape=jax.ShapeDtypeStruct((quads, 2, pairs, sub_dev, 2 * samples), bf16),
        compiler_params=pltpu.CompilerParams(vmem_limit_bytes=32 << 20),
        name="degrid",
    )(home, cuts, offs)

    groups = [[b * ffts + 2 * x + c for b in range(beams) for x in range(pairs)] for c in range(2)]
    parts = partial.reshape(beams * pairs, sub_dev, 2 * samples)
    came = lax.all_to_all(parts, axes, 0, 0, tiled=True, axis_index_groups=groups)
    total = jnp.sum(came.astype(f32), axis=0)
    total = lax.ppermute(total, axes, turn(0)) * (1.0 / image_side)
    total = total.reshape(sub_dev, 2, samples)

    mine = lambda a: lax.dynamic_slice_in_dim(a, my_fft * sub_dev, sub_dev, 0)
    base_hot = (mine(sub_base[0])[:, None] == jnp.arange(gain_table.shape[1], dtype=jnp.int32)[None, :]).astype(f32)
    gains = jnp.dot(base_hot, gain_table.T, precision=highest)
    g0, g1 = gains[:, 0:1], gains[:, 1:2]
    re = total[:, 0]
    im = jnp.where(mine(mirrored)[:, None], -total[:, 1], total[:, 1])
    return jnp.stack([g0 * re - g1 * im, g0 * im + g1 * re], axis=1)[None]


def solution(mesh):
    return jax.shard_map(
        local,
        mesh=mesh,
        in_specs=(
            P("beam", "fft", None), P(), P("beam", None, None, None), P("beam"),
            P("beam", None, None), P("beam", None), P("beam", None),
            P("beam", None, None, None), P("beam", None), P(),
        ),
        out_specs=P("beam", "fft", None, None),
        check_vma=False,
    )
```

```python
import functools
import math

import jax
import jax.numpy as jnp
from jax import lax
from jax.experimental import pallas as pl
from jax.experimental.pallas import tpu as pltpu
from jax.sharding import PartitionSpec as P

FT = 8
SG = 32
CAP = 8
LANES = 128

kernel_width = 1.5
highest = lax.Precision.HIGHEST
f32 = jnp.float32
bf16 = jnp.bfloat16


def round_up(number, unit):
    return -(-number // unit) * unit


def unit_phase(residue, period):
    angle = residue.astype(f32) * (2.0 * math.pi / period)
    return jnp.cos(angle), -jnp.sin(angle)


def split_phase(coarse, fine, col, period):
    cr, ci = unit_phase(fine * jnp.arange(coarse, dtype=jnp.int32)[:, None] * col % period, period)
    fr, fi = unit_phase(jnp.arange(fine, dtype=jnp.int32)[:, None] * col % period, period)
    cr, ci, fr, fi = cr[:, None], ci[:, None], fr[None], fi[None]
    return (cr * fr - ci * fi).reshape(-1, col.shape[0]), (cr * fi + ci * fr).reshape(-1, col.shape[0])


def window_kernel(
    ffts_ref, tix_ref, ti_ref, tj_ref, valid_ref, r0_ref, c0_ref, wr_ref, wi_ref,
    own_ref, oth_ref, prof_ref, flip_ref,
    tcos_ref, tsin_ref, lr0_ref, li0_ref, lr1_ref, li1_ref,
    ar_ref, ai_ref, br_ref, bi_ref,
    g_ref, rs_ref, low_ref, *, ffts, unroll,
):
    q = pl.program_id(0)
    side = own_ref.shape[2]
    half_side = side // 2
    per_tile = side // LANES
    per_half = per_tile // 2
    first_v = FT * ffts

    def prof_row(at):
        return prof_ref[0, pl.ds(at, 1), :]

    low_prof = jnp.concatenate(
        [prof_ref[0, pl.ds(first_v + p, FT, stride=per_tile), :] for p in range(per_half)], axis=1)
    low_ref[...] = jnp.dot(
        low_prof, flip_ref[...].astype(f32), precision=highest, preferred_element_type=f32)

    def some_tiles(step, carry):
        even, odd, row_scales = [], [], []
        for n in range(2):
            k = step * 2 + n
            t, i, j = tix_ref[q, k], ti_ref[q, k], tj_ref[q, k]
            scale_hi = jnp.concatenate(
                [prof_row(first_v + j * per_tile + p) for p in range(per_half, per_tile)], axis=1)
            scale_lo = low_ref[pl.ds(j, 1), :]
            lo = jnp.dot(
                jnp.concatenate([own_ref[t, :, :half_side], oth_ref[t, :, :half_side]], axis=0),
                flip_ref[...], preferred_element_type=f32) * scale_lo
            hi = jnp.concatenate(
                [own_ref[t, :, half_side:], oth_ref[t, :, half_side:]], axis=0).astype(f32) * scale_hi
            even.append((hi + lo).astype(bf16))
            odd.append((hi - lo).astype(bf16))
            for h in range(2):
                row_scales.append(prof_row(i * ffts + ffts_ref[h]) * valid_ref[q, k])
        row_scale = jnp.concatenate(row_scales, axis=1)
        for c, (table, parts) in enumerate(((tcos_ref, even), (tsin_ref, odd))):
            got = lax.dot_general(
                table[...], jnp.concatenate(parts, axis=0), (((1,), (1,)), ((), ())),
                preferred_element_type=f32,
            ) * row_scale
            for n in range(2):
                for h in range(2):
                    at = (2 * n + h) * LANES
                    rs_ref[h * 2 + c, step * 2 + n] = got[:, at:at + LANES]
        return carry

    lax.fori_loop(0, CAP // 2, some_tiles, 0)

    lane = lax.broadcasted_iota(jnp.int32, (2 * SG, LANES), 1)
    is_low = (lane // SG) == 1

    def one_sub(s):
        r0 = r0_ref[q, s]
        c0 = c0_ref[q, s]
        windows = jnp.concatenate([
            jnp.concatenate([rs_ref[j, k, pl.ds(c0, SG), :].astype(bf16) for j in range(4)], axis=1)
            for k in range(CAP)
        ], axis=0)
        lr0, li0, lr1, li1 = (
            ref[pl.ds(r0, SG), :].astype(bf16) for ref in (lr0_ref, li0_ref, lr1_ref, li1_ref))
        left = jnp.concatenate([
            jnp.concatenate([lr0, -li0, lr1, -li1], axis=1),
            jnp.concatenate([li0, lr0, li1, lr1], axis=1),
        ], axis=0)
        out = lax.dot_general(left, windows, (((1,), (1,)), ((), ())), preferred_element_type=f32)
        r8, c8 = lax.rem(r0, 8), lax.rem(c0, 8)
        ar, ai = (
            jnp.concatenate([ref[0, p, pl.ds(r8, 8), :] for p in range(2)], axis=1)
            for ref in (ar_ref, ai_ref))
        br, bi = br_ref[0, pl.ds(c8, 1), :], bi_ref[0, pl.ds(c8, 1), :]
        wr, wi = wr_ref[q, s], wi_ref[q, s]
        br, bi = br * wr - bi * wi, br * wi + bi * wr
        fr = ar * br - ai * bi
        fi = ar * bi + ai * br
        re_parts, im_parts = [], []
        for a in range(SG // 8):
            re = out[a * 8:(a + 1) * 8]
            im = out[SG + a * 8:SG + (a + 1) * 8]
            re_parts.append(re * fr - im * fi)
            im_parts.append(re * fi + im * fr)
        full = jnp.concatenate(re_parts + im_parts, axis=0)
        half = full[:, :LANES] + full[:, LANES:]
        half = half + pltpu.roll(half, 2 * SG, 1)
        half = half + pltpu.roll(half, SG, 1)
        high = half.astype(bf16)
        low = half - high.astype(f32)
        g_ref[0, s] = jnp.where(is_low, low, half).astype(bf16)

    def some_subs(i, carry):
        for u in range(unroll):
            one_sub(i * unroll + u)
        return carry

    lax.fori_loop(0, r0_ref.shape[1] // unroll, some_subs, 0)


def degrid_kernel(turn_ref, g_ref, off_ref, out_ref, acc_ref, *, unroll):
    subs = g_ref.shape[1]
    samples = off_ref.shape[3]
    places = lax.broadcasted_iota(jnp.int32, (SG, samples), 0).astype(f32)
    factor = -math.log2(math.e) / kernel_width**2
    blank = jnp.zeros((LANES - 3 * SG, samples), bf16)

    def one_sub(s):
        tu = places - off_ref[0, s, 0:1, :]
        tv = places - off_ref[0, s, 1:2, :]
        wu = jnp.exp2(tu * tu * factor)
        wv = jnp.exp2(tv * tv * factor)
        wv_high = wv.astype(bf16)
        wv_low = (wv - wv_high.astype(f32)).astype(bf16)
        right = jnp.concatenate([wv_high, wv_high, wv_low, blank], axis=0)
        inner = jnp.dot(g_ref[0, s], right, preferred_element_type=f32)
        re = jnp.sum(inner[:SG] * wu, axis=0, keepdims=True)
        im = jnp.sum(inner[SG:] * wu, axis=0, keepdims=True)
        acc_ref[pl.ds(s, 1), :] = jnp.concatenate([re, im], axis=1)

    def some_subs(i, carry):
        for u in range(unroll):
            one_sub(i * unroll + u)
        return carry

    lax.fori_loop(0, subs // unroll, some_subs, 0)
    out_ref[0, 0, 0] = acc_ref[...].astype(out_ref.dtype)


def local(
    sky_model, footprint, profile, chan_block, sub_strip, sub_row, sub_col,
    offsets, sub_base, gain_table,
):
    axes = ("beam", "fft")
    beams = lax.axis_size("beam")
    ffts = lax.axis_size("fft")
    my_beam = lax.axis_index("beam")
    my_fft = lax.axis_index("fft")
    my_core = my_fft % 2
    quads = beams // 2
    pairs = ffts // 2
    tiles_dev, tile_rows, tile_side = sky_model.shape
    image_side = FT * tile_side
    half_side = image_side // 2
    subs = sub_row.shape[1]
    sub_dev = subs // ffts
    samples = offsets.shape[3]
    strip_cols = image_side // ffts

    def turn(step):
        out = []
        for b in range(beams):
            for f in range(ffts):
                target = (2 * ((b // 2 - step) % quads) + f % 2) * ffts + 2 * (f // 2) + b % 2
                out.append((b * ffts + f, target))
        return out

    oth_sky = lax.ppermute(sky_model, "fft", [(f, f ^ 1) for f in range(ffts)])

    chosen = lax.dynamic_index_in_dim(profile[0], chan_block[0], 0, keepdims=False)
    col_at = sub_strip[0, :, 0] * strip_cols + sub_col[0]
    mirrored = col_at >= half_side
    r0_mine = jnp.where(mirrored, (image_side - (SG - 1) - sub_row[0]) % image_side, sub_row[0])
    c0_mine = jnp.where(mirrored, image_side - (SG - 1) - col_at, col_at)
    off_mine = jnp.where(mirrored[:, None, None], (SG - 1) - offsets[0], offsets[0])
    prof_u = jnp.pad(chosen[0].reshape(FT * ffts, tile_rows), ((0, 0), (0, LANES - tile_rows)))
    small = jnp.concatenate([
        prof_u, chosen[1].reshape(-1, LANES),
        r0_mine.astype(f32).reshape(-1, LANES), c0_mine.astype(f32).reshape(-1, LANES)])
    smalls = jnp.stack([lax.ppermute(small, axes, turn(t)) for t in range(quads)])
    offs = [lax.ppermute(off_mine, axes, turn(t)) for t in range(quads)]
    beam_ids = jnp.stack([2 * ((my_beam // 2 + t) % quads) + my_core for t in range(quads)])
    prof_rows = FT * ffts + image_side // LANES
    sub_rows = subs // LANES
    r0_all = smalls[:, prof_rows:prof_rows + sub_rows].reshape(quads, subs).astype(jnp.int32)
    c0_all = smalls[:, prof_rows + sub_rows:].reshape(quads, subs).astype(jnp.int32)

    lists = jnp.take(footprint, beam_ids, axis=0)
    hits = (lists // tiles_dev == my_beam).astype(jnp.int32)
    order = jnp.cumsum(hits, axis=1) - 1
    slots = hits[:, :, None] * (order[:, :, None] == jnp.arange(CAP, dtype=jnp.int32)[None, None, :])
    tix = jnp.sum(slots * (lists % tiles_dev)[:, :, None], axis=1)
    place = jnp.sum(slots * jnp.arange(FT * FT, dtype=jnp.int32)[None, :, None], axis=1)
    valid = jnp.sum(slots, axis=1).astype(f32)
    tile_i, tile_j = place // FT, place % FT
    fft_ids = jnp.stack([my_fft, my_fft + 1 - 2 * my_core])

    eights = jnp.arange(FT, dtype=jnp.int32)
    lane_e = jnp.arange(CAP * SG, dtype=jnp.int32) % SG
    lane_i = jnp.repeat(tile_i, SG, axis=1).reshape(quads, 2, 1, LANES)
    lane_j = jnp.repeat(tile_j, SG, axis=1)[:, None, :]
    ar, ai = unit_phase(lane_i * jnp.arange(16, dtype=jnp.int32)[:, None] % FT, FT)
    middle = 2 * image_side
    br, bi = unit_phase(
        (middle // FT * lane_j * (eights[:, None] + lane_e) + (tile_side - 1) * lane_e) % middle, middle)
    wr, wi = unit_phase((tile_side - 1) * c0_all % middle, middle)

    side_half = tile_side // 2
    t_cos, t_sin = split_phase(129, 16, 2 * jnp.arange(side_half, dtype=jnp.int32) + 1, middle)
    t_cos, t_sin = t_cos.astype(bf16), t_sin.astype(bf16)
    v_rows = t_cos.shape[0]
    left = []
    for h in range(2):
        col = fft_ids[h] * tile_rows + jnp.arange(LANES, dtype=jnp.int32)
        left += split_phase((image_side + SG) // SG, SG, col, image_side)
    place_z = jnp.arange(side_half, dtype=jnp.int32)
    flip = (place_z[:, None] + place_z[None, :] == side_half - 1).astype(bf16)
    if tile_rows < LANES:
        pad_rows = ((0, 0), (0, LANES - tile_rows), (0, 0))
        sky_model, oth_sky = jnp.pad(sky_model, pad_rows), jnp.pad(oth_sky, pad_rows)

    whole = lambda a: pl.BlockSpec(a.shape, lambda q, *_: (0,) * a.ndim, pipeline_mode=pl.Buffered(1))
    per_beam = lambda a: pl.BlockSpec((1,) + a.shape[1:], lambda q, *_: (q,) + (0,) * (a.ndim - 1))
    fixed = [flip, t_cos, t_sin, *left]
    phases = [ar, ai, br, bi]
    operands = [sky_model, oth_sky, smalls, *fixed, *phases]
    specs = [whole(sky_model), whole(oth_sky), per_beam(smalls)]
    specs += [whole(x) for x in fixed] + [per_beam(x) for x in phases]
    cuts = pl.pallas_call(
        functools.partial(window_kernel, ffts=ffts, unroll=16),
        out_shape=jax.ShapeDtypeStruct((quads, subs, 2 * SG, LANES), bf16),
        grid_spec=pltpu.PrefetchScalarGridSpec(
            num_scalar_prefetch=9, grid=(quads,), in_specs=specs,
            out_specs=pl.BlockSpec((1, subs, 2 * SG, LANES), lambda q, *_: (q, 0, 0, 0)),
            scratch_shapes=[pltpu.VMEM((4, CAP, v_rows, LANES), f32), pltpu.VMEM((FT, side_half), f32)],
        ),
        compiler_params=pltpu.CompilerParams(vmem_limit_bytes=63 << 20),
        name="windows",
    )(fft_ids, tix, tile_i, tile_j, valid, r0_all, c0_all, wr, wi, *operands)

    offs, cuts = lax.optimization_barrier((offs, cuts))
    offs = jnp.stack(offs)
    home = (my_beam // 2).astype(jnp.int32).reshape(1)
    partial = pl.pallas_call(
        functools.partial(degrid_kernel, unroll=8),
        grid_spec=pltpu.PrefetchScalarGridSpec(
            num_scalar_prefetch=1, grid=(quads, ffts),
            in_specs=[
                pl.BlockSpec((1, sub_dev, 2 * SG, LANES), lambda q, f, _: (q, f, 0, 0)),
                pl.BlockSpec((1, sub_dev, 2, samples), lambda q, f, _: (q, f, 0, 0)),
            ],
            out_specs=pl.BlockSpec(
                (1, 1, 1, sub_dev, 2 * samples),
                lambda q, f, home: (lax.rem(q + home[0], quads), lax.rem(f, 2), f // 2, 0, 0)),
            scratch_shapes=[pltpu.VMEM((sub_dev, 2 * samples), f32)],
        ),
        out_shape=jax.ShapeDtypeStruct((quads, 2, pairs, sub_dev, 2 * samples), bf16),
        compiler_params=pltpu.CompilerParams(vmem_limit_bytes=32 << 20),
        name="degrid",
    )(home, cuts, offs)

    groups = [[b * ffts + 2 * x + c for b in range(beams) for x in range(pairs)] for c in range(2)]
    parts = partial.reshape(beams * pairs, sub_dev, 2 * samples)
    came = lax.all_to_all(parts, axes, 0, 0, tiled=True, axis_index_groups=groups)
    total = jnp.sum(came.astype(f32), axis=0)
    total = lax.ppermute(total, axes, turn(0)) * (1.0 / image_side)
    total = total.reshape(sub_dev, 2, samples)

    mine = lambda a: lax.dynamic_slice_in_dim(a, my_fft * sub_dev, sub_dev, 0)
    base_hot = (mine(sub_base[0])[:, None] == jnp.arange(gain_table.shape[1], dtype=jnp.int32)[None, :]).astype(f32)
    gains = jnp.dot(base_hot, gain_table.T, precision=highest)
    g0, g1 = gains[:, 0:1], gains[:, 1:2]
    re = total[:, 0]
    im = jnp.where(mine(mirrored)[:, None], -total[:, 1], total[:, 1])
    return jnp.stack([g0 * re - g1 * im, g0 * im + g1 * re], axis=1)[None]


def solution(mesh):
    return jax.shard_map(
        local,
        mesh=mesh,
        in_specs=(
            P("beam", "fft", None), P(), P("beam", None, None, None), P("beam"),
            P("beam", None, None), P("beam", None), P("beam", None),
            P("beam", None, None, None), P("beam", None), P(),
        ),
        out_specs=P("beam", "fft", None, None),
        check_vma=False,
    )
```

```python
import functools
import math

import jax
import jax.numpy as jnp
import numpy as np
from jax import lax
from jax.experimental import pallas as pl
from jax.experimental.pallas import tpu as pltpu
from jax.sharding import PartitionSpec as P

FT = 8
SG = 32
CAP = 8
LANES = 128
OFF_LEAST, OFF_MOST = 2.0, 29.0
OFF_STEP = (OFF_MOST - OFF_LEAST) / 65535.0

kernel_width = 1.5
highest = lax.Precision.HIGHEST
f32 = jnp.float32
bf16 = jnp.bfloat16


def phase_table(rows, cols, period):
    angle = np.asarray(rows * cols % period) * (2.0 * math.pi / period)
    return jnp.asarray(np.stack([np.cos(angle), -np.sin(angle)]).astype(np.float32))


def turn_by(xr, xi, yr, yi):
    return xr * yr - xi * yi, xr * yi + xi * yr


def window_kernel(
    lists_ref, r0_ref, c0_ref, wr_ref, wi_ref,
    own_ref, oth_ref, prof_ref, v_coarse_ref, v_fine_ref, u_coarse_ref, u_fine_ref, ea_ref, eb_ref,
    *rest, beams, ffts, quads, unroll,
):
    off_refs, rest = rest[:quads], rest[quads:]
    (out_ref, rs_ref, low_ref, flip_ref, tcos_ref, tsin_ref, left_ref,
     a_ref, b_ref, off_ref, acc_ref, slot_ref) = rest
    q = pl.program_id(0)
    my_beam = lax.axis_index("beam")
    my_fft = lax.axis_index("fft")
    my_core = lax.rem(my_fft, 2)
    fft_ids = (my_fft, my_fft + 1 - 2 * my_core)
    quad = lax.rem(my_beam // 2 + q, quads)
    beam = 2 * quad + my_core
    tiles_dev = own_ref.shape[0]
    half_side = own_ref.shape[2] // 2
    per_half = half_side // LANES
    per_tile = 2 * per_half
    first_v = FT * ffts
    fine_v, fine_u = v_fine_ref.shape[1], u_fine_ref.shape[2]

    @pl.when(q == 0)
    def _():
        row = lax.broadcasted_iota(jnp.int32, (half_side, half_side), 0)
        col = lax.broadcasted_iota(jnp.int32, (half_side, half_side), 1)
        flip_ref[...] = (row + col == half_side - 1).astype(f32).astype(bf16)

        def some_rows(i, carry):
            for n in range(3):
                a = i * 3 + n
                cos, sin = turn_by(
                    v_coarse_ref[0, pl.ds(a, 1), :], v_coarse_ref[1, pl.ds(a, 1), :],
                    v_fine_ref[0], v_fine_ref[1])
                at = pl.ds(pl.multiple_of(a * fine_v, fine_v), fine_v)
                tcos_ref[at, :] = cos.astype(bf16)
                tsin_ref[at, :] = sin.astype(bf16)
                at = pl.ds(pl.multiple_of(a * fine_u, fine_u), fine_u)
                for h, f in enumerate(fft_ids):
                    cos, sin = turn_by(
                        u_coarse_ref[0, f, pl.ds(a, 1), :], u_coarse_ref[1, f, pl.ds(a, 1), :],
                        u_fine_ref[0, f], u_fine_ref[1, f])
                    left_ref[2 * h, at, :] = cos
                    left_ref[2 * h + 1, at, :] = sin
            return carry

        lax.fori_loop(0, v_coarse_ref.shape[1] // 3, some_rows, 0)

    for k in range(CAP):
        for n in range(3):
            slot_ref[n, k] = 0

    def one_entry(p, found):
        tile = lists_ref[beam, p]
        hit = (tile // tiles_dev) == my_beam

        @pl.when(hit)
        def _():
            at = jnp.minimum(found, CAP - 1)
            slot_ref[0, at] = lax.rem(tile, tiles_dev)
            slot_ref[1, at] = p // FT
            slot_ref[2, at] = lax.rem(p, FT)

        return found + hit.astype(jnp.int32)

    found = lax.fori_loop(0, FT * FT, one_entry, 0, unroll=8)

    lane = lax.broadcasted_iota(jnp.int32, (16, LANES), 1)
    for part in range(2):
        for half in range(2):
            a_rows, b_rows = ea_ref[part, 0], eb_ref[part, 0]
            for n in range(CAP // 2):
                here = lane // SG == n
                k = half * (CAP // 2) + n
                a_rows = jnp.where(here, ea_ref[part, slot_ref[1, k]], a_rows)
                b_rows = jnp.where(here[:8], eb_ref[part, slot_ref[2, k]], b_rows)
            a_ref[part, half] = a_rows
            b_ref[part, half] = b_rows

    for t in range(quads):
        @pl.when(q == t)
        def _():
            code = off_refs[t][...].astype(jnp.int32).astype(f32)
            off_ref[...] = (code + 32768.0) * OFF_STEP + OFF_LEAST

    def prof_row(at):
        return prof_ref[0, pl.ds(at, 1), :]

    low_prof = jnp.concatenate(
        [prof_ref[0, pl.ds(first_v + p, FT, stride=per_tile), :] for p in range(per_half)], axis=1)
    low_ref[...] = jnp.dot(
        low_prof, flip_ref[...].astype(f32), precision=highest, preferred_element_type=f32)

    def some_tiles(step, carry):
        even, odd, row_scales = [], [], []
        for n in range(2):
            k = step * 2 + n
            t, i, j = slot_ref[0, k], slot_ref[1, k], slot_ref[2, k]
            valid = (k < found).astype(f32)
            scale_hi = jnp.concatenate(
                [prof_row(first_v + j * per_tile + p) for p in range(per_half, per_tile)], axis=1)
            scale_lo = low_ref[pl.ds(j, 1), :]
            lo = jnp.dot(
                jnp.concatenate([own_ref[t, :, :half_side], oth_ref[t, :, :half_side]], axis=0),
                flip_ref[...], preferred_element_type=f32) * scale_lo
            hi = jnp.concatenate(
                [own_ref[t, :, half_side:], oth_ref[t, :, half_side:]], axis=0).astype(f32) * scale_hi
            even.append((hi + lo).astype(bf16))
            odd.append((hi - lo).astype(bf16))
            for f in fft_ids:
                row_scales.append(prof_row(i * ffts + f) * valid)
        row_scale = jnp.concatenate(row_scales, axis=1)
        for c, (table, parts) in enumerate(((tcos_ref, even), (tsin_ref, odd))):
            got = lax.dot_general(
                table[...], jnp.concatenate(parts, axis=0), (((1,), (1,)), ((), ())),
                preferred_element_type=f32,
            ) * row_scale
            for n in range(2):
                for h in range(2):
                    at = (2 * n + h) * LANES
                    rs_ref[h * 2 + c, step * 2 + n] = got[:, at:at + LANES]
        return carry

    lax.fori_loop(0, CAP // 2, some_tiles, 0)

    samples = off_ref.shape[1]
    wide = lax.broadcasted_iota(jnp.int32, (2 * SG, LANES), 1)
    is_low = (wide // SG) == 1
    places = lax.broadcasted_iota(jnp.int32, (SG, samples), 0).astype(f32)
    factor = -math.log2(math.e) / kernel_width**2
    blank = jnp.zeros((LANES - 3 * SG, samples), bf16)

    def one_sub(s):
        r0 = r0_ref[q, s]
        code = c0_ref[q, s]
        mirrored = code >= 2 * FT * half_side
        c0 = jnp.where(mirrored, code - 2 * FT * half_side, code)
        windows = jnp.concatenate([
            jnp.concatenate([rs_ref[j, k, pl.ds(c0, SG), :].astype(bf16) for j in range(4)], axis=1)
            for k in range(CAP)
        ], axis=0)
        lr0, li0, lr1, li1 = (left_ref[n, pl.ds(r0, SG), :].astype(bf16) for n in range(4))
        left = jnp.concatenate([
            jnp.concatenate([lr0, -li0, lr1, -li1], axis=1),
            jnp.concatenate([li0, lr0, li1, lr1], axis=1),
        ], axis=0)
        out = lax.dot_general(left, windows, (((1,), (1,)), ((), ())), preferred_element_type=f32)
        r8, c8 = lax.rem(r0, 8), lax.rem(c0, 8)
        ar, ai = (
            jnp.concatenate([a_ref[part, half, pl.ds(r8, 8), :] for half in range(2)], axis=1)
            for part in range(2))
        br, bi = (
            jnp.concatenate([b_ref[part, half, pl.ds(c8, 1), :] for half in range(2)], axis=1)
            for part in range(2))
        br, bi = turn_by(br, bi, wr_ref[q, s], wi_ref[q, s])
        fr, fi = turn_by(ar, ai, br, bi)
        re_parts, im_parts = [], []
        for a in range(SG // 8):
            re, im = turn_by(out[a * 8:(a + 1) * 8], out[SG + a * 8:SG + (a + 1) * 8], fr, fi)
            re_parts.append(re)
            im_parts.append(im)
        full = jnp.concatenate(re_parts + im_parts, axis=0)
        half = full[:, :LANES] + full[:, LANES:]
        half = half + pltpu.roll(half, 2 * SG, 1)
        half = half + pltpu.roll(half, SG, 1)
        low = half - half.astype(bf16).astype(f32)
        cut = jnp.where(is_low, low, half).astype(bf16)

        base = jnp.where(mirrored, SG - 1.0, 0.0)
        way = jnp.where(mirrored, -1.0, 1.0)
        at = places * way + base
        tu = at - off_ref[pl.ds(2 * s, 1), :]
        tv = at - off_ref[pl.ds(2 * s + 1, 1), :]
        wu = jnp.exp2(tu * tu * factor)
        wv = jnp.exp2(tv * tv * factor)
        wv_high = wv.astype(bf16)
        wv_low = (wv - wv_high.astype(f32)).astype(bf16)
        right = jnp.concatenate([wv_high, wv_high, wv_low, blank], axis=0)
        inner = jnp.dot(cut, right, preferred_element_type=f32)
        re = jnp.sum(inner[:SG] * wu, axis=0, keepdims=True)
        im = jnp.sum(inner[SG:] * wu, axis=0, keepdims=True)
        acc_ref[pl.ds(s, 1), :] = jnp.concatenate([re, im], axis=1)

    def some_subs(i, carry):
        for u in range(unroll):
            one_sub(i * unroll + u)
        return carry

    subs = acc_ref.shape[0]
    lax.fori_loop(0, subs // unroll, some_subs, 0)
    sub_dev = subs // ffts
    for f in range(ffts):
        out_ref[quad, f % 2, f // 2] = acc_ref[f * sub_dev:(f + 1) * sub_dev].astype(out_ref.dtype)


def local(
    sky_model, footprint, profile, chan_block, sub_strip, sub_row, sub_col,
    offsets, sub_base, gain_table,
):
    axes = ("beam", "fft")
    beams = lax.axis_size("beam")
    ffts = lax.axis_size("fft")
    my_fft = lax.axis_index("fft")
    quads = beams // 2
    pairs = ffts // 2
    tiles_dev, tile_rows, tile_side = sky_model.shape
    image_side = FT * tile_side
    half_side = image_side // 2
    subs = sub_row.shape[1]
    sub_dev = subs // ffts
    samples = offsets.shape[3]
    strip_cols = image_side // ffts

    def turn(step):
        out = []
        for b in range(beams):
            for f in range(ffts):
                target = (2 * ((b // 2 - step) % quads) + f % 2) * ffts + 2 * (f // 2) + b % 2
                out.append((b * ffts + f, target))
        return out

    oth_sky = lax.ppermute(sky_model, "fft", [(f, f ^ 1) for f in range(ffts)])

    chosen = lax.dynamic_index_in_dim(profile[0], chan_block[0], 0, keepdims=False)
    col_at = sub_strip[0, :, 0] * strip_cols + sub_col[0]
    mirrored = col_at >= half_side
    r0_mine = jnp.where(mirrored, (image_side - (SG - 1) - sub_row[0]) % image_side, sub_row[0])
    c0_mine = jnp.where(mirrored, image_side - (SG - 1) - col_at, col_at)
    middle = 2 * image_side
    angle = ((tile_side - 1) * c0_mine % middle).astype(f32) * (2.0 * math.pi / middle)
    code_mine = jnp.where(mirrored, c0_mine + image_side, c0_mine)
    prof_u = jnp.pad(chosen[0].reshape(FT * ffts, tile_rows), ((0, 0), (0, LANES - tile_rows)))
    per_sub = [r0_mine.astype(f32), code_mine.astype(f32), jnp.cos(angle), -jnp.sin(angle)]
    small = jnp.concatenate(
        [prof_u, chosen[1].reshape(-1, LANES)] + [x.reshape(-1, LANES) for x in per_sub])
    smalls = jnp.stack([lax.ppermute(small, axes, turn(t)) for t in range(quads)])
    off_code = jnp.round((offsets[0].reshape(2 * subs, samples) - OFF_LEAST) * (1.0 / OFF_STEP)) - 32768.0
    off_code = off_code.astype(jnp.int16)
    offs = [lax.ppermute(off_code, axes, turn(t)) for t in range(quads)]
    sub_parts = smalls[:, FT * ffts + image_side // LANES:].reshape(quads, 4, subs)
    r0_all, c0_all = sub_parts[:, 0].astype(jnp.int32), sub_parts[:, 1].astype(jnp.int32)
    wr, wi = sub_parts[:, 2], sub_parts[:, 3]

    side_half = tile_side // 2
    coarse, fine_v, fine_u = 129, image_side // 256, SG
    v_col = 2 * np.arange(side_half) + 1
    v_coarse = phase_table(fine_v * np.arange(coarse)[:, None], v_col, middle)
    v_fine = phase_table(np.arange(fine_v)[:, None], v_col, middle)
    u_col = np.arange(ffts)[:, None, None] * tile_rows + np.arange(LANES)
    u_coarse = phase_table(fine_u * np.arange(coarse)[:, None], u_col, image_side)
    u_fine = phase_table(np.arange(fine_u)[:, None], u_col, image_side)
    lane_e = np.arange(LANES) % SG
    eights = np.arange(FT)[:, None, None]
    ea = phase_table(eights * np.arange(16)[:, None], np.ones(LANES, np.int64), FT)
    eb = phase_table(
        middle // FT * eights * (np.arange(8)[:, None] + lane_e) + (tile_side - 1) * lane_e, 1, middle)
    v_rows, u_rows = coarse * fine_v, coarse * fine_u
    if tile_rows < LANES:
        pad_rows = ((0, 0), (0, LANES - tile_rows), (0, 0))
        sky_model, oth_sky = jnp.pad(sky_model, pad_rows), jnp.pad(oth_sky, pad_rows)

    whole = lambda a: pl.BlockSpec(a.shape, lambda q, *_: (0,) * a.ndim, pipeline_mode=pl.Buffered(1))
    per_beam = lambda a: pl.BlockSpec((1,) + a.shape[1:], lambda q, *_: (q,) + (0,) * (a.ndim - 1))
    fixed = [v_coarse, v_fine, u_coarse, u_fine, ea, eb, *offs]
    out_shape = (quads, 2, pairs, sub_dev, 2 * samples)
    partial = pl.pallas_call(
        functools.partial(window_kernel, beams=beams, ffts=ffts, quads=quads, unroll=8),
        out_shape=jax.ShapeDtypeStruct(out_shape, bf16),
        grid_spec=pltpu.PrefetchScalarGridSpec(
            num_scalar_prefetch=5, grid=(quads,),
            in_specs=[whole(sky_model), whole(oth_sky), per_beam(smalls)] + [whole(x) for x in fixed],
            out_specs=pl.BlockSpec(out_shape, lambda q, *_: (0,) * len(out_shape)),
            scratch_shapes=[
                pltpu.VMEM((4, CAP, v_rows, LANES), f32),
                pltpu.VMEM((FT, side_half), f32),
                pltpu.VMEM((side_half, side_half), bf16),
                pltpu.VMEM((v_rows, side_half), bf16),
                pltpu.VMEM((v_rows, side_half), bf16),
                pltpu.VMEM((4, u_rows, LANES), f32),
                pltpu.VMEM((2, 2, 16, LANES), f32),
                pltpu.VMEM((2, 2, 8, LANES), f32),
                pltpu.VMEM((2 * subs, samples), f32),
                pltpu.VMEM((subs, 2 * samples), f32),
                pltpu.SMEM((3, CAP), jnp.int32),
            ],
        ),
        compiler_params=pltpu.CompilerParams(vmem_limit_bytes=63 << 20),
        name="windows",
    )(footprint, r0_all, c0_all, wr, wi, sky_model, oth_sky, smalls, *fixed)

    groups = [[b * ffts + 2 * x + c for b in range(beams) for x in range(pairs)] for c in range(2)]
    parts = partial.reshape(beams * pairs, sub_dev, 2 * samples)
    came = lax.all_to_all(parts, axes, 0, 0, tiled=True, axis_index_groups=groups)
    total = jnp.sum(came.astype(f32), axis=0)
    total = lax.ppermute(total, axes, turn(0)) * (1.0 / image_side)
    total = total.reshape(sub_dev, 2, samples)

    mine = lambda a: lax.dynamic_slice_in_dim(a, my_fft * sub_dev, sub_dev, 0)
    base_hot = (mine(sub_base[0])[:, None] == jnp.arange(gain_table.shape[1], dtype=jnp.int32)[None, :]).astype(f32)
    gains = jnp.dot(base_hot, gain_table.T, precision=highest)
    g0, g1 = gains[:, 0:1], gains[:, 1:2]
    re = total[:, 0]
    im = jnp.where(mine(mirrored)[:, None], -total[:, 1], total[:, 1])
    return jnp.stack([g0 * re - g1 * im, g0 * im + g1 * re], axis=1)[None]


def solution(mesh):
    return jax.shard_map(
        local,
        mesh=mesh,
        in_specs=(
            P("beam", "fft", None), P(), P("beam", None, None, None), P("beam"),
            P("beam", None, None), P("beam", None), P("beam", None),
            P("beam", None, None, None), P("beam", None), P(),
        ),
        out_specs=P("beam", "fft", None, None),
        check_vma=False,
    )
```

```python
import functools
import math

import jax
import jax.numpy as jnp
import numpy as np
from jax import lax
from jax.experimental import pallas as pl
from jax.experimental.pallas import tpu as pltpu
from jax.sharding import PartitionSpec as P

FT = 8
SG = 32
CAP = 8
LANES = 128
OFF_LEAST, OFF_MOST = 2.0, 29.0
OFF_STEP = (OFF_MOST - OFF_LEAST) / 65535.0

kernel_width = 1.5
highest = lax.Precision.HIGHEST
f32 = jnp.float32
bf16 = jnp.bfloat16


def phase_table(rows, cols, period):
    angle = np.asarray(rows * cols % period) * (2.0 * math.pi / period)
    return jnp.asarray(np.stack([np.cos(angle), -np.sin(angle)]).astype(np.float32))


def turn_by(xr, xi, yr, yi):
    return xr * yr - xi * yi, xr * yi + xi * yr


def window_kernel(
    lists_ref, r0_ref, c0_ref, wr_ref, wi_ref,
    own_ref, oth_ref, prof_ref, v_coarse_ref, v_fine_ref, u_coarse_ref, u_fine_ref, ea_ref, eb_ref,
    *rest, beams, ffts, quads, unroll,
):
    off_refs, rest = rest[:quads], rest[quads:]
    (out_ref, rs_ref, low_ref, flip_ref, tcos_ref, tsin_ref, left_ref,
     a_ref, b_ref, off_ref, acc_ref, slot_ref) = rest
    q = pl.program_id(0)
    my_beam = lax.axis_index("beam")
    my_fft = lax.axis_index("fft")
    my_core = lax.rem(my_fft, 2)
    fft_ids = (my_fft, my_fft + 1 - 2 * my_core)
    quad = lax.rem(my_beam // 2 + q, quads)
    beam = 2 * quad + my_core
    tiles_dev = own_ref.shape[0]
    half_side = own_ref.shape[2] // 2
    per_half = half_side // LANES
    per_tile = 2 * per_half
    first_v = FT * ffts
    fine_v, fine_u = v_fine_ref.shape[1], u_fine_ref.shape[2]

    @pl.when(q == 0)
    def _():
        row = lax.broadcasted_iota(jnp.int32, (half_side, half_side), 0)
        col = lax.broadcasted_iota(jnp.int32, (half_side, half_side), 1)
        flip_ref[...] = (row + col == half_side - 1).astype(f32).astype(bf16)

        def some_rows(i, carry):
            for n in range(3):
                a = i * 3 + n
                cos, sin = turn_by(
                    v_coarse_ref[0, pl.ds(a, 1), :], v_coarse_ref[1, pl.ds(a, 1), :],
                    v_fine_ref[0], v_fine_ref[1])
                at = pl.ds(pl.multiple_of(a * fine_v, fine_v), fine_v)
                tcos_ref[at, :] = cos.astype(bf16)
                tsin_ref[at, :] = sin.astype(bf16)
                at = pl.ds(pl.multiple_of(a * fine_u, fine_u), fine_u)
                for h, f in enumerate(fft_ids):
                    cos, sin = turn_by(
                        u_coarse_ref[0, f, pl.ds(a, 1), :], u_coarse_ref[1, f, pl.ds(a, 1), :],
                        u_fine_ref[0, f], u_fine_ref[1, f])
                    left_ref[2 * h, at, :] = cos
                    left_ref[2 * h + 1, at, :] = sin
            return carry

        lax.fori_loop(0, v_coarse_ref.shape[1] // 3, some_rows, 0)

    for k in range(CAP):
        for n in range(3):
            slot_ref[n, k] = 0

    def one_entry(p, found):
        tile = lists_ref[beam, p]
        hit = (tile // tiles_dev) == my_beam

        @pl.when(hit)
        def _():
            at = jnp.minimum(found, CAP - 1)
            slot_ref[0, at] = lax.rem(tile, tiles_dev)
            slot_ref[1, at] = p // FT
            slot_ref[2, at] = lax.rem(p, FT)

        return found + hit.astype(jnp.int32)

    found = lax.fori_loop(0, FT * FT, one_entry, 0, unroll=16)

    lane = lax.broadcasted_iota(jnp.int32, (16, LANES), 1)
    for part in range(2):
        for half in range(2):
            a_rows, b_rows = ea_ref[part, 0], eb_ref[part, 0]
            for n in range(CAP // 2):
                here = lane // SG == n
                k = half * (CAP // 2) + n
                a_rows = jnp.where(here, ea_ref[part, slot_ref[1, k]], a_rows)
                b_rows = jnp.where(here[:8], eb_ref[part, slot_ref[2, k]], b_rows)
            a_ref[part, half] = a_rows
            b_ref[part, half] = b_rows

    for t in range(quads):
        @pl.when(q == t)
        def _():
            code = off_refs[t][...].astype(jnp.int32).astype(f32)
            off_ref[...] = (code + 32768.0) * OFF_STEP + OFF_LEAST

    def prof_row(at):
        return prof_ref[0, pl.ds(at, 1), :]

    low_prof = jnp.concatenate(
        [prof_ref[0, pl.ds(first_v + p, FT, stride=per_tile), :] for p in range(per_half)], axis=1)
    low_ref[...] = jnp.dot(
        low_prof, flip_ref[...].astype(f32), precision=highest, preferred_element_type=f32)

    def some_tiles(step, carry):
        even, odd, row_scales = [], [], []
        for n in range(2):
            k = step * 2 + n
            t, i, j = slot_ref[0, k], slot_ref[1, k], slot_ref[2, k]
            valid = (k < found).astype(f32)
            scale_hi = jnp.concatenate(
                [prof_row(first_v + j * per_tile + p) for p in range(per_half, per_tile)], axis=1)
            scale_lo = low_ref[pl.ds(j, 1), :]
            lo = jnp.dot(
                jnp.concatenate([own_ref[t, :, :half_side], oth_ref[t, :, :half_side]], axis=0),
                flip_ref[...], preferred_element_type=f32) * scale_lo
            hi = jnp.concatenate(
                [own_ref[t, :, half_side:], oth_ref[t, :, half_side:]], axis=0).astype(f32) * scale_hi
            even.append((hi + lo).astype(bf16))
            odd.append((hi - lo).astype(bf16))
            for f in fft_ids:
                row_scales.append(prof_row(i * ffts + f) * valid)
        row_scale = jnp.concatenate(row_scales, axis=1)
        for c, (table, parts) in enumerate(((tcos_ref, even), (tsin_ref, odd))):
            got = lax.dot_general(
                table[...], jnp.concatenate(parts, axis=0), (((1,), (1,)), ((), ())),
                preferred_element_type=f32,
            ) * row_scale
            for n in range(2):
                for h in range(2):
                    at = (2 * n + h) * LANES
                    rs_ref[h * 2 + c, step * 2 + n] = got[:, at:at + LANES]
        return carry

    lax.fori_loop(0, CAP // 2, some_tiles, 0)

    samples = off_ref.shape[1]
    wide = lax.broadcasted_iota(jnp.int32, (2 * SG, LANES), 1)
    is_low = (wide // SG) == 1
    places = lax.broadcasted_iota(jnp.int32, (SG, samples), 0).astype(f32)
    factor = -math.log2(math.e) / kernel_width**2
    blank = jnp.zeros((LANES - 3 * SG, samples), bf16)

    def cut_out(s):
        r0 = r0_ref[q, s]
        code = c0_ref[q, s]
        mirrored = code >= 2 * FT * half_side
        c0 = jnp.where(mirrored, code - 2 * FT * half_side, code)
        windows = jnp.concatenate([
            jnp.concatenate([rs_ref[j, k, pl.ds(c0, SG), :].astype(bf16) for j in range(4)], axis=1)
            for k in range(CAP)
        ], axis=0)
        lr0, li0, lr1, li1 = (left_ref[n, pl.ds(r0, SG), :].astype(bf16) for n in range(4))
        left = jnp.concatenate([
            jnp.concatenate([lr0, -li0, lr1, -li1], axis=1),
            jnp.concatenate([li0, lr0, li1, lr1], axis=1),
        ], axis=0)
        out = lax.dot_general(left, windows, (((1,), (1,)), ((), ())), preferred_element_type=f32)
        r8, c8 = lax.rem(r0, 8), lax.rem(c0, 8)
        ar, ai = (
            jnp.concatenate([a_ref[part, half, pl.ds(r8, 8), :] for half in range(2)], axis=1)
            for part in range(2))
        br, bi = (
            jnp.concatenate([b_ref[part, half, pl.ds(c8, 1), :] for half in range(2)], axis=1)
            for part in range(2))
        br, bi = turn_by(br, bi, wr_ref[q, s], wi_ref[q, s])
        fr, fi = turn_by(ar, ai, br, bi)
        re_parts, im_parts = [], []
        for a in range(SG // 8):
            re, im = turn_by(out[a * 8:(a + 1) * 8], out[SG + a * 8:SG + (a + 1) * 8], fr, fi)
            re_parts.append(re)
            im_parts.append(im)
        full = jnp.concatenate(re_parts + im_parts, axis=0)
        half = full[:, :LANES] + full[:, LANES:]
        half = half + pltpu.roll(half, 2 * SG, 1)
        half = half + pltpu.roll(half, SG, 1)
        low = half - half.astype(bf16).astype(f32)
        return jnp.where(is_low, low, half).astype(bf16)

    def degrid(s, cut):
        mirrored = c0_ref[q, s] >= 2 * FT * half_side
        base = jnp.where(mirrored, SG - 1.0, 0.0)
        way = jnp.where(mirrored, -1.0, 1.0)
        at = places * way + base
        tu = at - off_ref[pl.ds(2 * s, 1), :]
        tv = at - off_ref[pl.ds(2 * s + 1, 1), :]
        wu = jnp.exp2(tu * tu * factor)
        wv = jnp.exp2(tv * tv * factor)
        wv_high = wv.astype(bf16)
        wv_low = (wv - wv_high.astype(f32)).astype(bf16)
        right = jnp.concatenate([wv_high, wv_high, wv_low, blank], axis=0)
        inner = jnp.dot(cut, right, preferred_element_type=f32)
        re = jnp.sum(inner[:SG] * wu, axis=0, keepdims=True)
        im = jnp.sum(inner[SG:] * wu, axis=0, keepdims=True)
        return jnp.concatenate([re, im], axis=1)

    def some_subs(i, carry):
        cuts = [cut_out(i * unroll + u) for u in range(unroll)]
        rows = [degrid(i * unroll + u, cuts[u]) for u in range(unroll)]
        acc_ref[pl.ds(pl.multiple_of(i * unroll, unroll), unroll), :] = jnp.concatenate(rows, axis=0)
        return carry

    subs = acc_ref.shape[0]
    lax.fori_loop(0, subs // unroll, some_subs, 0)
    sub_dev = subs // ffts
    for f in range(ffts):
        out_ref[quad, f % 2, f // 2] = acc_ref[f * sub_dev:(f + 1) * sub_dev].astype(out_ref.dtype)


def local(
    sky_model, footprint, profile, chan_block, sub_strip, sub_row, sub_col,
    offsets, sub_base, gain_table,
):
    axes = ("beam", "fft")
    beams = lax.axis_size("beam")
    ffts = lax.axis_size("fft")
    my_fft = lax.axis_index("fft")
    quads = beams // 2
    pairs = ffts // 2
    tiles_dev, tile_rows, tile_side = sky_model.shape
    image_side = FT * tile_side
    half_side = image_side // 2
    subs = sub_row.shape[1]
    sub_dev = subs // ffts
    samples = offsets.shape[3]
    strip_cols = image_side // ffts

    def turn(step):
        out = []
        for b in range(beams):
            for f in range(ffts):
                target = (2 * ((b // 2 - step) % quads) + f % 2) * ffts + 2 * (f // 2) + b % 2
                out.append((b * ffts + f, target))
        return out

    oth_sky = lax.ppermute(sky_model, "fft", [(f, f ^ 1) for f in range(ffts)])

    chosen = lax.dynamic_index_in_dim(profile[0], chan_block[0], 0, keepdims=False)
    col_at = sub_strip[0, :, 0] * strip_cols + sub_col[0]
    mirrored = col_at >= half_side
    r0_mine = jnp.where(mirrored, (image_side - (SG - 1) - sub_row[0]) % image_side, sub_row[0])
    c0_mine = jnp.where(mirrored, image_side - (SG - 1) - col_at, col_at)
    middle = 2 * image_side
    angle = ((tile_side - 1) * c0_mine % middle).astype(f32) * (2.0 * math.pi / middle)
    code_mine = jnp.where(mirrored, c0_mine + image_side, c0_mine)
    prof_u = jnp.pad(chosen[0].reshape(FT * ffts, tile_rows), ((0, 0), (0, LANES - tile_rows)))
    per_sub = [r0_mine.astype(f32), code_mine.astype(f32), jnp.cos(angle), -jnp.sin(angle)]
    small = jnp.concatenate(
        [prof_u, chosen[1].reshape(-1, LANES)] + [x.reshape(-1, LANES) for x in per_sub])
    smalls = jnp.stack([lax.ppermute(small, axes, turn(t)) for t in range(quads)])
    off_code = jnp.round((offsets[0].reshape(2 * subs, samples) - OFF_LEAST) * (1.0 / OFF_STEP)) - 32768.0
    off_code = off_code.astype(jnp.int16)
    offs = [lax.ppermute(off_code, axes, turn(t)) for t in range(quads)]
    sub_parts = smalls[:, FT * ffts + image_side // LANES:].reshape(quads, 4, subs)
    r0_all, c0_all = sub_parts[:, 0].astype(jnp.int32), sub_parts[:, 1].astype(jnp.int32)
    wr, wi = sub_parts[:, 2], sub_parts[:, 3]

    side_half = tile_side // 2
    coarse, fine_v, fine_u = 129, image_side // 256, SG
    v_col = 2 * np.arange(side_half) + 1
    v_coarse = phase_table(fine_v * np.arange(coarse)[:, None], v_col, middle)
    v_fine = phase_table(np.arange(fine_v)[:, None], v_col, middle)
    u_col = np.arange(ffts)[:, None, None] * tile_rows + np.arange(LANES)
    u_coarse = phase_table(fine_u * np.arange(coarse)[:, None], u_col, image_side)
    u_fine = phase_table(np.arange(fine_u)[:, None], u_col, image_side)
    lane_e = np.arange(LANES) % SG
    eights = np.arange(FT)[:, None, None]
    ea = phase_table(eights * np.arange(16)[:, None], np.ones(LANES, np.int64), FT)
    eb = phase_table(
        middle // FT * eights * (np.arange(8)[:, None] + lane_e) + (tile_side - 1) * lane_e, 1, middle)
    v_rows, u_rows = coarse * fine_v, coarse * fine_u
    if tile_rows < LANES:
        pad_rows = ((0, 0), (0, LANES - tile_rows), (0, 0))
        sky_model, oth_sky = jnp.pad(sky_model, pad_rows), jnp.pad(oth_sky, pad_rows)

    whole = lambda a: pl.BlockSpec(a.shape, lambda q, *_: (0,) * a.ndim, pipeline_mode=pl.Buffered(1))
    per_beam = lambda a: pl.BlockSpec((1,) + a.shape[1:], lambda q, *_: (q,) + (0,) * (a.ndim - 1))
    fixed = [v_coarse, v_fine, u_coarse, u_fine, ea, eb, *offs]
    out_shape = (quads, 2, pairs, sub_dev, 2 * samples)
    partial = pl.pallas_call(
        functools.partial(window_kernel, beams=beams, ffts=ffts, quads=quads, unroll=16),
        out_shape=jax.ShapeDtypeStruct(out_shape, bf16),
        grid_spec=pltpu.PrefetchScalarGridSpec(
            num_scalar_prefetch=5, grid=(quads,),
            in_specs=[whole(sky_model), whole(oth_sky), per_beam(smalls)] + [whole(x) for x in fixed],
            out_specs=pl.BlockSpec(out_shape, lambda q, *_: (0,) * len(out_shape)),
            scratch_shapes=[
                pltpu.VMEM((4, CAP, v_rows, LANES), f32),
                pltpu.VMEM((FT, side_half), f32),
                pltpu.VMEM((side_half, side_half), bf16),
                pltpu.VMEM((v_rows, side_half), bf16),
                pltpu.VMEM((v_rows, side_half), bf16),
                pltpu.VMEM((4, u_rows, LANES), f32),
                pltpu.VMEM((2, 2, 16, LANES), f32),
                pltpu.VMEM((2, 2, 8, LANES), f32),
                pltpu.VMEM((2 * subs, samples), f32),
                pltpu.VMEM((subs, 2 * samples), f32),
                pltpu.SMEM((3, CAP), jnp.int32),
            ],
        ),
        compiler_params=pltpu.CompilerParams(vmem_limit_bytes=63 << 20),
        name="windows",
    )(footprint, r0_all, c0_all, wr, wi, sky_model, oth_sky, smalls, *fixed)

    groups = [[b * ffts + 2 * x + c for b in range(beams) for x in range(pairs)] for c in range(2)]
    parts = partial.reshape(beams * pairs, sub_dev, 2 * samples)
    came = lax.all_to_all(parts, axes, 0, 0, tiled=True, axis_index_groups=groups)
    total = jnp.sum(came.astype(f32), axis=0)
    total = lax.ppermute(total, axes, turn(0)) * (1.0 / image_side)
    total = total.reshape(sub_dev, 2, samples)

    mine = lambda a: lax.dynamic_slice_in_dim(a, my_fft * sub_dev, sub_dev, 0)
    base_hot = (mine(sub_base[0])[:, None] == jnp.arange(gain_table.shape[1], dtype=jnp.int32)[None, :]).astype(f32)
    gains = jnp.dot(base_hot, gain_table.T, precision=highest)
    g0, g1 = gains[:, 0:1], gains[:, 1:2]
    re = total[:, 0]
    im = jnp.where(mine(mirrored)[:, None], -total[:, 1], total[:, 1])
    return jnp.stack([g0 * re - g1 * im, g0 * im + g1 * re], axis=1)[None]


def solution(mesh):
    return jax.shard_map(
        local,
        mesh=mesh,
        in_specs=(
            P("beam", "fft", None), P(), P("beam", None, None, None), P("beam"),
            P("beam", None, None), P("beam", None), P("beam", None),
            P("beam", None, None, None), P("beam", None), P(),
        ),
        out_specs=P("beam", "fft", None, None),
        check_vma=False,
    )
```

```python
import functools
import math

import jax
import jax.numpy as jnp
import numpy as np
from jax import lax
from jax.experimental import pallas as pl
from jax.experimental.pallas import tpu as pltpu
from jax.sharding import PartitionSpec as P

FT = 8
SG = 32
CAP = 8
LANES = 128
OFF_LEAST, OFF_MOST = 2.0, 29.0
PROF_UNIT = 2.0**25
OFF_STEP = (OFF_MOST - OFF_LEAST) / 65535.0

kernel_width = 1.5
highest = lax.Precision.HIGHEST
f32 = jnp.float32
bf16 = jnp.bfloat16


def phase_table(rows, cols, period):
    angle = np.asarray(rows * cols % period) * (2.0 * math.pi / period)
    return jnp.asarray(np.stack([np.cos(angle), -np.sin(angle)]).astype(np.float32))


def turn_by(xr, xi, yr, yi):
    return xr * yr - xi * yi, xr * yi + xi * yr


def window_kernel(
    tix_ref, ti_ref, tj_ref, valid_ref, r0_ref, c0_ref, wr_ref, wi_ref,
    own_ref, oth_ref, v_coarse_ref, v_fine_ref, u_coarse_ref, u_fine_ref, ea_ref, eb_ref,
    *rest, ffts, quads, unroll,
):
    small_refs, rest = rest[:quads], rest[quads:]
    (out_ref, rs_ref, low_ref, flip_ref, prof_ref, off_ref, acc_ref,
     tcos_ref, tsin_ref, left_ref, a_ref, b_ref) = rest
    q = pl.program_id(0)
    my_beam = lax.axis_index("beam")
    my_fft = lax.axis_index("fft")
    my_core = lax.rem(my_fft, 2)
    fft_ids = (my_fft, my_fft + 1 - 2 * my_core)
    fine_v, fine_u = v_fine_ref.shape[1], u_fine_ref.shape[2]
    quad = lax.rem(my_beam // 2 + q, quads)
    half_side = own_ref.shape[2] // 2
    per_half = half_side // LANES
    per_tile = 2 * per_half
    first_v = FT * ffts
    subs = acc_ref.shape[0]
    prof_rows = prof_ref.shape[0]
    off_at = prof_rows + 4 * (subs // LANES)

    @pl.when(q == 0)
    def _():
        row = lax.broadcasted_iota(jnp.int32, (half_side, half_side), 0)
        col = lax.broadcasted_iota(jnp.int32, (half_side, half_side), 1)
        flip_ref[...] = (row + col == half_side - 1).astype(f32).astype(bf16)

        def some_rows(i, carry):
            for n in range(3):
                a = i * 3 + n
                cos, sin = turn_by(
                    v_coarse_ref[0, pl.ds(a, 1), :], v_coarse_ref[1, pl.ds(a, 1), :],
                    v_fine_ref[0], v_fine_ref[1])
                at = pl.ds(pl.multiple_of(a * fine_v, fine_v), fine_v)
                tcos_ref[at, :] = cos.astype(bf16)
                tsin_ref[at, :] = sin.astype(bf16)
                at = pl.ds(pl.multiple_of(a * fine_u, fine_u), fine_u)
                for h, f in enumerate(fft_ids):
                    cos, sin = turn_by(
                        u_coarse_ref[0, f, pl.ds(a, 1), :], u_coarse_ref[1, f, pl.ds(a, 1), :],
                        u_fine_ref[0, f], u_fine_ref[1, f])
                    left_ref[2 * h, at, :] = cos
                    left_ref[2 * h + 1, at, :] = sin
            return carry

        lax.fori_loop(0, v_coarse_ref.shape[1] // 3, some_rows, 0)

    lane = lax.broadcasted_iota(jnp.int32, (16, LANES), 1)
    for part in range(2):
        for half in range(2):
            a_rows, b_rows = ea_ref[part, 0], eb_ref[part, 0]
            for n in range(CAP // 2):
                here = lane // SG == n
                k = half * (CAP // 2) + n
                a_rows = jnp.where(here, ea_ref[part, ti_ref[q, k]], a_rows)
                b_rows = jnp.where(here[:8], eb_ref[part, tj_ref[q, k]], b_rows)
            a_ref[part, half] = a_rows
            b_ref[part, half] = b_rows

    for t in range(quads):
        @pl.when(q == t)
        def _():
            prof_ref[...] = small_refs[t][:prof_rows].astype(f32) * (1.0 / PROF_UNIT)
            for h in range(off_ref.shape[2] // LANES):
                code = small_refs[t][off_at + h * subs:off_at + (h + 1) * subs]
                pair = ((code & 65535).astype(f32), (code >> 16).astype(f32) + 32768.0)
                for n in range(2):
                    off_ref[n, :, h * LANES:(h + 1) * LANES] = pair[n] * OFF_STEP + OFF_LEAST

    def prof_row(at):
        return prof_ref[pl.ds(at, 1), :]

    low_prof = jnp.concatenate(
        [prof_ref[pl.ds(first_v + p, FT, stride=per_tile), :] for p in range(per_half)], axis=1)
    low_ref[...] = jnp.dot(
        low_prof, flip_ref[...].astype(f32), precision=highest, preferred_element_type=f32)

    def some_tiles(step, carry):
        even, odd, row_scales = [], [], []
        for n in range(2):
            k = step * 2 + n
            t, i, j = tix_ref[q, k], ti_ref[q, k], tj_ref[q, k]
            valid = valid_ref[q, k].astype(f32)
            scale_hi = jnp.concatenate(
                [prof_row(first_v + j * per_tile + p) for p in range(per_half, per_tile)], axis=1)
            scale_lo = low_ref[pl.ds(j, 1), :]
            lo = jnp.dot(
                jnp.concatenate([own_ref[t, :, :half_side], oth_ref[t, :, :half_side]], axis=0),
                flip_ref[...], preferred_element_type=f32) * scale_lo
            hi = jnp.concatenate(
                [own_ref[t, :, half_side:], oth_ref[t, :, half_side:]], axis=0).astype(f32) * scale_hi
            even.append((hi + lo).astype(bf16))
            odd.append((hi - lo).astype(bf16))
            for f in fft_ids:
                row_scales.append(prof_row(i * ffts + f) * valid)
        row_scale = jnp.concatenate(row_scales, axis=1)
        for c, (table, parts) in enumerate(((tcos_ref, even), (tsin_ref, odd))):
            got = lax.dot_general(
                table[...], jnp.concatenate(parts, axis=0), (((1,), (1,)), ((), ())),
                preferred_element_type=f32,
            ) * row_scale
            for n in range(2):
                for h in range(2):
                    at = (2 * n + h) * LANES
                    rs_ref[h * 2 + c, step * 2 + n] = got[:, at:at + LANES]
        return carry

    lax.fori_loop(0, CAP // 2, some_tiles, 0)

    samples = off_ref.shape[2]
    wide = lax.broadcasted_iota(jnp.int32, (2 * SG, LANES), 1)
    is_low = (wide // SG) == 1
    places = lax.broadcasted_iota(jnp.int32, (SG, samples), 0).astype(f32)
    factor = -math.log2(math.e) / kernel_width**2

    def cut_out(s):
        r0 = r0_ref[q, s]
        code = c0_ref[q, s]
        mirrored = code >= 2 * FT * half_side
        c0 = jnp.where(mirrored, code - 2 * FT * half_side, code)
        windows = jnp.concatenate([
            jnp.concatenate([rs_ref[j, k, pl.ds(c0, SG), :].astype(bf16) for j in range(4)], axis=1)
            for k in range(CAP)
        ], axis=0)
        lr0, li0, lr1, li1 = (left_ref[n, pl.ds(r0, SG), :].astype(bf16) for n in range(4))
        left = jnp.concatenate([
            jnp.concatenate([lr0, -li0, lr1, -li1], axis=1),
            jnp.concatenate([li0, lr0, li1, lr1], axis=1),
        ], axis=0)
        out = lax.dot_general(left, windows, (((1,), (1,)), ((), ())), preferred_element_type=f32)
        r8, c8 = lax.rem(r0, 8), lax.rem(c0, 8)
        ar, ai = (
            jnp.concatenate([a_ref[part, half, pl.ds(r8, 8), :] for half in range(2)], axis=1)
            for part in range(2))
        br, bi = (
            jnp.concatenate([b_ref[part, half, pl.ds(c8, 1), :] for half in range(2)], axis=1)
            for part in range(2))
        br, bi = turn_by(br, bi, wr_ref[q, s], wi_ref[q, s])
        fr, fi = turn_by(ar, ai, br, bi)
        re_parts, im_parts = [], []
        for a in range(SG // 8):
            re, im = turn_by(out[a * 8:(a + 1) * 8], out[SG + a * 8:SG + (a + 1) * 8], fr, fi)
            re_parts.append(re)
            im_parts.append(im)
        full = jnp.concatenate(re_parts + im_parts, axis=0)
        half = full[:, :LANES] + full[:, LANES:]
        half = half + pltpu.roll(half, 2 * SG, 1)
        half = half + pltpu.roll(half, SG, 1)
        low = half - half.astype(bf16).astype(f32)
        return jnp.where(is_low, low, half).astype(bf16)

    def degrid(s, cut):
        mirrored = c0_ref[q, s] >= 2 * FT * half_side
        base = jnp.where(mirrored, SG - 1.0, 0.0)
        way = jnp.where(mirrored, -1.0, 1.0)
        at = places * way + base
        tu = at - off_ref[0, pl.ds(s, 1), :]
        tv = at - off_ref[1, pl.ds(s, 1), :]
        wu = jnp.exp2(tu * tu * factor)
        wv = jnp.exp2(tv * tv * factor)
        wv_high = wv.astype(bf16)
        wv_low = (wv - wv_high.astype(f32)).astype(bf16)
        right = jnp.concatenate([wv_high, wv_high, wv_low], axis=0)
        inner = jnp.dot(cut[:, :3 * SG], right, preferred_element_type=f32)
        re = jnp.sum(inner[:SG] * wu, axis=0, keepdims=True)
        im = jnp.sum(inner[SG:] * wu, axis=0, keepdims=True)
        return jnp.concatenate([re, im], axis=1)

    def some_subs(i, carry):
        cuts = [cut_out(i * unroll + u) for u in range(unroll)]
        rows = [degrid(i * unroll + u, cuts[u]) for u in range(unroll)]
        acc_ref[pl.ds(pl.multiple_of(i * unroll, unroll), unroll), :] = jnp.concatenate(rows, axis=0)
        return carry

    lax.fori_loop(0, subs // unroll, some_subs, 0)
    sub_dev = subs // ffts
    for f in range(ffts):
        out_ref[quad, f % 2, f // 2] = acc_ref[f * sub_dev:(f + 1) * sub_dev].astype(out_ref.dtype)


def local(
    sky_model, footprint, profile, chan_block, sub_strip, sub_row, sub_col,
    offsets, sub_base, gain_table,
):
    axes = ("beam", "fft")
    beams = lax.axis_size("beam")
    ffts = lax.axis_size("fft")
    my_fft = lax.axis_index("fft")
    quads = beams // 2
    pairs = ffts // 2
    tiles_dev, tile_rows, tile_side = sky_model.shape
    image_side = FT * tile_side
    half_side = image_side // 2
    subs = sub_row.shape[1]
    sub_dev = subs // ffts
    samples = offsets.shape[3]
    strip_cols = image_side // ffts

    def turn(step):
        out = []
        for b in range(beams):
            for f in range(ffts):
                target = (2 * ((b // 2 - step) % quads) + f % 2) * ffts + 2 * (f // 2) + b % 2
                out.append((b * ffts + f, target))
        return out

    oth_sky = lax.ppermute(sky_model, "fft", [(f, f ^ 1) for f in range(ffts)])

    chosen = lax.dynamic_index_in_dim(profile[0], chan_block[0], 0, keepdims=False)
    col_at = sub_strip[0, :, 0] * strip_cols + sub_col[0]
    mirrored = col_at >= half_side
    r0_mine = jnp.where(mirrored, (image_side - (SG - 1) - sub_row[0]) % image_side, sub_row[0])
    c0_mine = jnp.where(mirrored, image_side - (SG - 1) - col_at, col_at)
    middle = 2 * image_side
    angle = ((tile_side - 1) * c0_mine % middle).astype(f32) * (2.0 * math.pi / middle)
    code_mine = jnp.where(mirrored, c0_mine + image_side, c0_mine)
    unit = 2.0**30
    per_sub = [r0_mine, code_mine] + [(x * unit).astype(jnp.int32) for x in (jnp.cos(angle), -jnp.sin(angle))]
    prof_int = (chosen * PROF_UNIT).astype(jnp.int32)
    prof_u = jnp.pad(prof_int[0].reshape(FT * ffts, tile_rows), ((0, 0), (0, LANES - tile_rows)))
    off_code = jnp.round((offsets[0] - OFF_LEAST) * (1.0 / OFF_STEP)).astype(jnp.int32)
    off_code = off_code[:, 0] + (off_code[:, 1] - 32768) * 65536
    small = jnp.concatenate(
        [prof_u, prof_int[1].reshape(-1, LANES)] + [x.reshape(-1, LANES) for x in per_sub]
        + [off_code[:, at:at + LANES] for at in range(0, samples, LANES)])
    smalls = [lax.ppermute(small, axes, turn(t)) for t in range(quads)]
    prof_rows = FT * ffts + image_side // LANES
    sub_rows = subs // LANES
    sub_parts = jnp.stack([x[prof_rows:prof_rows + 4 * sub_rows] for x in smalls]).reshape(quads, 4, subs)
    r0_all, c0_all = sub_parts[:, 0], sub_parts[:, 1]
    wr, wi = (sub_parts[:, n].astype(f32) * (1.0 / unit) for n in (2, 3))

    my_beam = lax.axis_index("beam")
    beam_ids = 2 * ((my_beam // 2 + jnp.arange(quads, dtype=jnp.int32)) % quads) + my_fft % 2
    pick_beam = beam_ids[:, None, None] == jnp.arange(beams, dtype=jnp.int32)[None, :, None]
    lists = jnp.sum(jnp.where(pick_beam, footprint[None], 0), axis=1)
    hits = lists // tiles_dev == my_beam
    entry = jnp.arange(FT * FT, dtype=jnp.int32)
    earlier = entry[None, :] < entry[:, None]
    order = jnp.sum(jnp.where(hits[:, None, :] & earlier[None], 1, 0), axis=2)
    slots = hits[:, None, :] & (order[:, None, :] == jnp.arange(CAP, dtype=jnp.int32)[None, :, None])
    in_slot = lambda values: jnp.sum(jnp.where(slots, values, 0), axis=2)
    tix = in_slot((lists % tiles_dev)[:, None, :])
    tile_i, tile_j = in_slot(entry // FT), in_slot(entry % FT)
    valid = in_slot(1)

    side_half = tile_side // 2
    coarse, fine_v, fine_u = 129, image_side // 256, SG
    v_col = 2 * np.arange(side_half) + 1
    v_coarse = phase_table(fine_v * np.arange(coarse)[:, None], v_col, middle)
    v_fine = phase_table(np.arange(fine_v)[:, None], v_col, middle)
    u_col = np.arange(ffts)[:, None, None] * tile_rows + np.arange(LANES)
    u_coarse = phase_table(fine_u * np.arange(coarse)[:, None], u_col, image_side)
    u_fine = phase_table(np.arange(fine_u)[:, None], u_col, image_side)
    lane_e = np.arange(LANES) % SG
    eights = np.arange(FT)[:, None, None]
    ea = phase_table(eights * np.arange(16)[:, None], np.ones(LANES, np.int64), FT)
    eb = phase_table(
        middle // FT * eights * (np.arange(8)[:, None] + lane_e) + (tile_side - 1) * lane_e, 1, middle)
    v_rows, u_rows = coarse * fine_v, coarse * fine_u
    if tile_rows < LANES:
        pad_rows = ((0, 0), (0, LANES - tile_rows), (0, 0))
        sky_model, oth_sky = jnp.pad(sky_model, pad_rows), jnp.pad(oth_sky, pad_rows)

    whole = lambda a: pl.BlockSpec(a.shape, lambda q, *_: (0,) * a.ndim, pipeline_mode=pl.Buffered(1))
    fixed = [sky_model, oth_sky, v_coarse, v_fine, u_coarse, u_fine, ea, eb, *smalls]
    out_shape = (quads, 2, pairs, sub_dev, 2 * samples)
    partial = pl.pallas_call(
        functools.partial(window_kernel, ffts=ffts, quads=quads, unroll=32),
        out_shape=jax.ShapeDtypeStruct(out_shape, bf16),
        grid_spec=pltpu.PrefetchScalarGridSpec(
            num_scalar_prefetch=8, grid=(quads,),
            in_specs=[whole(x) for x in fixed],
            out_specs=pl.BlockSpec(out_shape, lambda q, *_: (0,) * len(out_shape)),
            scratch_shapes=[
                pltpu.VMEM((4, CAP, v_rows, LANES), f32),
                pltpu.VMEM((FT, side_half), f32),
                pltpu.VMEM((side_half, side_half), bf16),
                pltpu.VMEM((prof_rows, LANES), f32),
                pltpu.VMEM((2, subs, samples), f32),
                pltpu.VMEM((subs, 2 * samples), f32),
                pltpu.VMEM((v_rows, side_half), bf16),
                pltpu.VMEM((v_rows, side_half), bf16),
                pltpu.VMEM((4, u_rows, LANES), f32),
                pltpu.VMEM((2, 2, 16, LANES), f32),
                pltpu.VMEM((2, 2, 8, LANES), f32),
            ],
        ),
        compiler_params=pltpu.CompilerParams(vmem_limit_bytes=63 << 20),
        name="windows",
    )(tix, tile_i, tile_j, valid, r0_all, c0_all, wr, wi, *fixed)

    groups = [[b * ffts + 2 * x + c for b in range(beams) for x in range(pairs)] for c in range(2)]
    parts = partial.reshape(beams * pairs, sub_dev, 2 * samples)
    came = lax.all_to_all(parts, axes, 0, 0, tiled=True, axis_index_groups=groups)
    total = jnp.sum(came.astype(f32), axis=0)
    total = lax.ppermute(total, axes, turn(0)) * (1.0 / image_side)
    total = total.reshape(sub_dev, 2, samples)

    mine = lambda a: lax.dynamic_slice_in_dim(a, my_fft * sub_dev, sub_dev, 0)
    base_hot = (mine(sub_base[0])[:, None] == jnp.arange(gain_table.shape[1], dtype=jnp.int32)[None, :]).astype(f32)
    gains = jnp.dot(base_hot, gain_table.T, precision=highest)
    g0, g1 = gains[:, 0:1], gains[:, 1:2]
    re = total[:, 0]
    im = jnp.where(mine(mirrored)[:, None], -total[:, 1], total[:, 1])
    return jnp.stack([g0 * re - g1 * im, g0 * im + g1 * re], axis=1)[None]


def solution(mesh):
    return jax.shard_map(
        local,
        mesh=mesh,
        in_specs=(
            P("beam", "fft", None), P(), P("beam", None, None, None), P("beam"),
            P("beam", None, None), P("beam", None), P("beam", None),
            P("beam", None, None, None), P("beam", None), P(),
        ),
        out_specs=P("beam", "fft", None, None),
        check_vma=False,
    )
```

```python
import functools
import math

import jax
import jax.numpy as jnp
import numpy as np
from jax import lax
from jax.experimental import pallas as pl
from jax.experimental.pallas import tpu as pltpu
from jax.sharding import PartitionSpec as P

FT = 8
SG = 32
CAP = 8
LANES = 128
LAG = 12
OFF_LEAST, OFF_MOST = 2.0, 29.0
PROF_UNIT = 2.0**25
OFF_STEP = (OFF_MOST - OFF_LEAST) / 65535.0

kernel_width = 1.5
highest = lax.Precision.HIGHEST
f32 = jnp.float32
bf16 = jnp.bfloat16


def phase_table(rows, cols, period):
    angle = np.asarray(rows * cols % period) * (2.0 * math.pi / period)
    return jnp.asarray(np.stack([np.cos(angle), -np.sin(angle)]).astype(np.float32))


def turn_by(xr, xi, yr, yi):
    return xr * yr - xi * yi, xr * yi + xi * yr


def window_kernel(
    tix_ref, ti_ref, tj_ref, valid_ref, r0_ref, c0_ref, wr_ref, wi_ref,
    own_ref, oth_ref, v_coarse_ref, v_fine_ref, u_coarse_ref, u_fine_ref, ea_ref, eb_ref,
    *rest, ffts, quads, unroll,
):
    small_refs, rest = rest[:quads], rest[quads:]
    (out_ref, rs_ref, low_ref, flip_ref, prof_ref, off_ref, acc_ref,
     tcos_ref, tsin_ref, left_ref, a_ref, b_ref) = rest
    q = pl.program_id(0)
    my_beam = lax.axis_index("beam")
    my_fft = lax.axis_index("fft")
    my_core = lax.rem(my_fft, 2)
    fft_ids = (my_fft, my_fft + 1 - 2 * my_core)
    fine_v, fine_u = v_fine_ref.shape[1], u_fine_ref.shape[2]
    quad = lax.rem(my_beam // 2 + q, quads)
    half_side = own_ref.shape[2] // 2
    per_half = half_side // LANES
    per_tile = 2 * per_half
    first_v = FT * ffts
    subs = acc_ref.shape[0]
    prof_rows = prof_ref.shape[0]
    off_at = prof_rows + 4 * (subs // LANES)

    @pl.when(q == 0)
    def _():
        row = lax.broadcasted_iota(jnp.int32, (half_side, half_side), 0)
        col = lax.broadcasted_iota(jnp.int32, (half_side, half_side), 1)
        flip_ref[...] = (row + col == half_side - 1).astype(f32).astype(bf16)

        def some_rows(i, carry):
            for n in range(3):
                a = i * 3 + n
                cos, sin = turn_by(
                    v_coarse_ref[0, pl.ds(a, 1), :], v_coarse_ref[1, pl.ds(a, 1), :],
                    v_fine_ref[0], v_fine_ref[1])
                at = pl.ds(pl.multiple_of(a * fine_v, fine_v), fine_v)
                tcos_ref[at, :] = cos.astype(bf16)
                tsin_ref[at, :] = sin.astype(bf16)
                at = pl.ds(pl.multiple_of(a * fine_u, fine_u), fine_u)
                for h, f in enumerate(fft_ids):
                    cos, sin = turn_by(
                        u_coarse_ref[0, f, pl.ds(a, 1), :], u_coarse_ref[1, f, pl.ds(a, 1), :],
                        u_fine_ref[0, f], u_fine_ref[1, f])
                    left_ref[2 * h, at, :] = cos
                    left_ref[2 * h + 1, at, :] = sin
            return carry

        lax.fori_loop(0, v_coarse_ref.shape[1] // 3, some_rows, 0)

    lane = lax.broadcasted_iota(jnp.int32, (16, LANES), 1)
    for part in range(2):
        for half in range(2):
            a_rows, b_rows = ea_ref[part, 0], eb_ref[part, 0]
            for n in range(CAP // 2):
                here = lane // SG == n
                k = half * (CAP // 2) + n
                a_rows = jnp.where(here, ea_ref[part, ti_ref[q, k]], a_rows)
                b_rows = jnp.where(here[:8], eb_ref[part, tj_ref[q, k]], b_rows)
            a_ref[part, half] = a_rows
            b_ref[part, half] = b_rows

    for t in range(quads):
        @pl.when(q == t)
        def _():
            prof_ref[...] = small_refs[t][:prof_rows].astype(f32) * (1.0 / PROF_UNIT)
            for h in range(off_ref.shape[2] // LANES):
                code = small_refs[t][off_at + h * subs:off_at + (h + 1) * subs]
                pair = ((code & 65535).astype(f32), (code >> 16).astype(f32) + 32768.0)
                for n in range(2):
                    off_ref[n, :, h * LANES:(h + 1) * LANES] = pair[n] * OFF_STEP + OFF_LEAST

    def prof_row(at):
        return prof_ref[pl.ds(at, 1), :]

    low_prof = jnp.concatenate(
        [prof_ref[pl.ds(first_v + p, FT, stride=per_tile), :] for p in range(per_half)], axis=1)
    low_ref[...] = jnp.dot(
        low_prof, flip_ref[...].astype(f32), precision=highest, preferred_element_type=f32)

    def some_tiles(step, carry):
        even, odd, row_scales = [], [], []
        for n in range(2):
            k = step * 2 + n
            t, i, j = tix_ref[q, k], ti_ref[q, k], tj_ref[q, k]
            valid = valid_ref[q, k].astype(f32)
            scale_hi = jnp.concatenate(
                [prof_row(first_v + j * per_tile + p) for p in range(per_half, per_tile)], axis=1)
            scale_lo = low_ref[pl.ds(j, 1), :]
            lo = jnp.dot(
                jnp.concatenate([own_ref[t, :, :half_side], oth_ref[t, :, :half_side]], axis=0),
                flip_ref[...], preferred_element_type=f32) * scale_lo
            hi = jnp.concatenate(
                [own_ref[t, :, half_side:], oth_ref[t, :, half_side:]], axis=0).astype(f32) * scale_hi
            even.append((hi + lo).astype(bf16))
            odd.append((hi - lo).astype(bf16))
            for f in fft_ids:
                row_scales.append(prof_row(i * ffts + f) * valid)
        row_scale = jnp.concatenate(row_scales, axis=1)
        for c, (table, parts) in enumerate(((tcos_ref, even), (tsin_ref, odd))):
            got = lax.dot_general(
                table[...], jnp.concatenate(parts, axis=0), (((1,), (1,)), ((), ())),
                preferred_element_type=f32,
            ) * row_scale
            for n in range(2):
                for h in range(2):
                    at = (2 * n + h) * LANES
                    rs_ref[h * 2 + c, step * 2 + n] = got[:, at:at + LANES]
        return carry

    for step in range(CAP // 2):
        some_tiles(step, 0)

    samples = off_ref.shape[2]
    wide = lax.broadcasted_iota(jnp.int32, (2 * SG, LANES), 1)
    is_low = (wide // SG) == 1
    places = lax.broadcasted_iota(jnp.int32, (SG, samples), 0).astype(f32)
    factor = -math.log2(math.e) / kernel_width**2

    def cut_out(s):
        r0 = r0_ref[q, s]
        code = c0_ref[q, s]
        mirrored = code >= 2 * FT * half_side
        c0 = jnp.where(mirrored, code - 2 * FT * half_side, code)
        windows = jnp.concatenate([
            jnp.concatenate([rs_ref[j, k, pl.ds(c0, SG), :].astype(bf16) for j in range(4)], axis=1)
            for k in range(CAP)
        ], axis=0)
        lr0, li0, lr1, li1 = (left_ref[n, pl.ds(r0, SG), :].astype(bf16) for n in range(4))
        left = jnp.concatenate([
            jnp.concatenate([lr0, -li0, lr1, -li1], axis=1),
            jnp.concatenate([li0, lr0, li1, lr1], axis=1),
        ], axis=0)
        out = lax.dot_general(left, windows, (((1,), (1,)), ((), ())), preferred_element_type=f32)
        r8, c8 = lax.rem(r0, 8), lax.rem(c0, 8)
        ar, ai = (
            jnp.concatenate([a_ref[part, half, pl.ds(r8, 8), :] for half in range(2)], axis=1)
            for part in range(2))
        br, bi = (
            jnp.concatenate([b_ref[part, half, pl.ds(c8, 1), :] for half in range(2)], axis=1)
            for part in range(2))
        br, bi = turn_by(br, bi, wr_ref[q, s], wi_ref[q, s])
        fr, fi = turn_by(ar, ai, br, bi)
        re_parts, im_parts = [], []
        for a in range(SG // 8):
            re, im = turn_by(out[a * 8:(a + 1) * 8], out[SG + a * 8:SG + (a + 1) * 8], fr, fi)
            re_parts.append(re)
            im_parts.append(im)
        full = jnp.concatenate(re_parts + im_parts, axis=0)
        half = full[:, :LANES] + full[:, LANES:]
        half = half + pltpu.roll(half, 2 * SG, 1)
        half = half + pltpu.roll(half, SG, 1)
        low = half - half.astype(bf16).astype(f32)
        return jnp.where(is_low, low, half).astype(bf16)

    def degrid(s, cut):
        mirrored = c0_ref[q, s] >= 2 * FT * half_side
        base = jnp.where(mirrored, SG - 1.0, 0.0)
        way = jnp.where(mirrored, -1.0, 1.0)
        at = places * way + base
        tu = at - off_ref[0, pl.ds(s, 1), :]
        tv = at - off_ref[1, pl.ds(s, 1), :]
        wu = jnp.exp2(tu * tu * factor)
        wv = jnp.exp2(tv * tv * factor)
        wv_high = wv.astype(bf16)
        wv_low = (wv - wv_high.astype(f32)).astype(bf16)
        right = jnp.concatenate([wv_high, wv_high, wv_low], axis=0)
        inner = jnp.dot(cut[:, :3 * SG], right, preferred_element_type=f32)
        re = jnp.sum(inner[:SG] * wu, axis=0, keepdims=True)
        im = jnp.sum(inner[SG:] * wu, axis=0, keepdims=True)
        return jnp.concatenate([re, im], axis=1)

    def some_subs(i, carry):
        cuts, rows = [], []
        for u in range(unroll + LAG):
            if u < unroll:
                cuts.append(cut_out(i * unroll + u))
            if u >= LAG:
                rows.append(degrid(i * unroll + u - LAG, cuts[u - LAG]))
        acc_ref[pl.ds(pl.multiple_of(i * unroll, unroll), unroll), :] = jnp.concatenate(rows, axis=0)
        return carry

    lax.fori_loop(0, subs // unroll, some_subs, 0)
    sub_dev = subs // ffts
    for f in range(ffts):
        out_ref[quad, f % 2, f // 2] = acc_ref[f * sub_dev:(f + 1) * sub_dev].astype(out_ref.dtype)


def local(
    sky_model, footprint, profile, chan_block, sub_strip, sub_row, sub_col,
    offsets, sub_base, gain_table,
):
    axes = ("beam", "fft")
    beams = lax.axis_size("beam")
    ffts = lax.axis_size("fft")
    my_fft = lax.axis_index("fft")
    quads = beams // 2
    pairs = ffts // 2
    tiles_dev, tile_rows, tile_side = sky_model.shape
    image_side = FT * tile_side
    half_side = image_side // 2
    subs = sub_row.shape[1]
    sub_dev = subs // ffts
    samples = offsets.shape[3]
    strip_cols = image_side // ffts

    def turn(step):
        out = []
        for b in range(beams):
            for f in range(ffts):
                target = (2 * ((b // 2 - step) % quads) + f % 2) * ffts + 2 * (f // 2) + b % 2
                out.append((b * ffts + f, target))
        return out

    oth_sky = lax.ppermute(sky_model, "fft", [(f, f ^ 1) for f in range(ffts)])

    chosen = lax.dynamic_index_in_dim(profile[0], chan_block[0], 0, keepdims=False)
    col_at = sub_strip[0, :, 0] * strip_cols + sub_col[0]
    mirrored = col_at >= half_side
    r0_mine = jnp.where(mirrored, (image_side - (SG - 1) - sub_row[0]) % image_side, sub_row[0])
    c0_mine = jnp.where(mirrored, image_side - (SG - 1) - col_at, col_at)
    middle = 2 * image_side
    angle = ((tile_side - 1) * c0_mine % middle).astype(f32) * (2.0 * math.pi / middle)
    code_mine = jnp.where(mirrored, c0_mine + image_side, c0_mine)
    unit = 2.0**30
    per_sub = [r0_mine, code_mine] + [(x * unit).astype(jnp.int32) for x in (jnp.cos(angle), -jnp.sin(angle))]
    prof_int = (chosen * PROF_UNIT).astype(jnp.int32)
    prof_u = jnp.pad(prof_int[0].reshape(FT * ffts, tile_rows), ((0, 0), (0, LANES - tile_rows)))
    off_code = jnp.round((offsets[0] - OFF_LEAST) * (1.0 / OFF_STEP)).astype(jnp.int32)
    off_code = off_code[:, 0] + (off_code[:, 1] - 32768) * 65536
    small = jnp.concatenate(
        [prof_u, prof_int[1].reshape(-1, LANES)] + [x.reshape(-1, LANES) for x in per_sub]
        + [off_code[:, at:at + LANES] for at in range(0, samples, LANES)])
    smalls = [lax.ppermute(small, axes, turn(t)) for t in range(quads)]
    prof_rows = FT * ffts + image_side // LANES
    sub_rows = subs // LANES
    sub_parts = jnp.stack([x[prof_rows:prof_rows + 4 * sub_rows] for x in smalls]).reshape(quads, 4, subs)
    r0_all, c0_all = sub_parts[:, 0], sub_parts[:, 1]
    wr, wi = (sub_parts[:, n].astype(f32) * (1.0 / unit) for n in (2, 3))

    my_beam = lax.axis_index("beam")
    beam_ids = 2 * ((my_beam // 2 + jnp.arange(quads, dtype=jnp.int32)) % quads) + my_fft % 2
    pick_beam = beam_ids[:, None, None] == jnp.arange(beams, dtype=jnp.int32)[None, :, None]
    lists = jnp.sum(jnp.where(pick_beam, footprint[None], 0), axis=1)
    hits = lists // tiles_dev == my_beam
    entry = jnp.arange(FT * FT, dtype=jnp.int32)
    earlier = entry[None, :] < entry[:, None]
    order = jnp.sum(jnp.where(hits[:, None, :] & earlier[None], 1, 0), axis=2)
    slots = hits[:, None, :] & (order[:, None, :] == jnp.arange(CAP, dtype=jnp.int32)[None, :, None])
    in_slot = lambda values: jnp.sum(jnp.where(slots, values, 0), axis=2)
    tix = in_slot((lists % tiles_dev)[:, None, :])
    tile_i, tile_j = in_slot(entry // FT), in_slot(entry % FT)
    valid = in_slot(1)

    side_half = tile_side // 2
    coarse, fine_v, fine_u = 129, image_side // 256, SG
    v_col = 2 * np.arange(side_half) + 1
    v_coarse = phase_table(fine_v * np.arange(coarse)[:, None], v_col, middle)
    v_fine = phase_table(np.arange(fine_v)[:, None], v_col, middle)
    u_col = np.arange(ffts)[:, None, None] * tile_rows + np.arange(LANES)
    u_coarse = phase_table(fine_u * np.arange(coarse)[:, None], u_col, image_side)
    u_fine = phase_table(np.arange(fine_u)[:, None], u_col, image_side)
    lane_e = np.arange(LANES) % SG
    eights = np.arange(FT)[:, None, None]
    ea = phase_table(eights * np.arange(16)[:, None], np.ones(LANES, np.int64), FT)
    eb = phase_table(
        middle // FT * eights * (np.arange(8)[:, None] + lane_e) + (tile_side - 1) * lane_e, 1, middle)
    v_rows, u_rows = coarse * fine_v, coarse * fine_u
    if tile_rows < LANES:
        pad_rows = ((0, 0), (0, LANES - tile_rows), (0, 0))
        sky_model, oth_sky = jnp.pad(sky_model, pad_rows), jnp.pad(oth_sky, pad_rows)

    whole = lambda a: pl.BlockSpec(a.shape, lambda q, *_: (0,) * a.ndim, pipeline_mode=pl.Buffered(1))
    fixed = [sky_model, oth_sky, v_coarse, v_fine, u_coarse, u_fine, ea, eb, *smalls]
    out_shape = (quads, 2, pairs, sub_dev, 2 * samples)
    partial = pl.pallas_call(
        functools.partial(window_kernel, ffts=ffts, quads=quads, unroll=64),
        out_shape=jax.ShapeDtypeStruct(out_shape, bf16),
        grid_spec=pltpu.PrefetchScalarGridSpec(
            num_scalar_prefetch=8, grid=(quads,),
            in_specs=[whole(x) for x in fixed],
            out_specs=pl.BlockSpec(out_shape, lambda q, *_: (0,) * len(out_shape)),
            scratch_shapes=[
                pltpu.VMEM((4, CAP, v_rows, LANES), f32),
                pltpu.VMEM((FT, side_half), f32),
                pltpu.VMEM((side_half, side_half), bf16),
                pltpu.VMEM((prof_rows, LANES), f32),
                pltpu.VMEM((2, subs, samples), f32),
                pltpu.VMEM((subs, 2 * samples), f32),
                pltpu.VMEM((v_rows, side_half), bf16),
                pltpu.VMEM((v_rows, side_half), bf16),
                pltpu.VMEM((4, u_rows, LANES), f32),
                pltpu.VMEM((2, 2, 16, LANES), f32),
                pltpu.VMEM((2, 2, 8, LANES), f32),
            ],
        ),
        compiler_params=pltpu.CompilerParams(vmem_limit_bytes=63 << 20),
        name="windows",
    )(tix, tile_i, tile_j, valid, r0_all, c0_all, wr, wi, *fixed)

    groups = [[b * ffts + 2 * x + c for b in range(beams) for x in range(pairs)] for c in range(2)]
    parts = partial.reshape(beams * pairs, sub_dev, 2 * samples)
    came = lax.all_to_all(parts, axes, 0, 0, tiled=True, axis_index_groups=groups)
    total = jnp.sum(came.astype(f32), axis=0)
    total = lax.ppermute(total, axes, turn(0)) * (1.0 / image_side)
    total = total.reshape(sub_dev, 2, samples)

    mine = lambda a: lax.dynamic_slice_in_dim(a, my_fft * sub_dev, sub_dev, 0)
    base_hot = (mine(sub_base[0])[:, None] == jnp.arange(gain_table.shape[1], dtype=jnp.int32)[None, :]).astype(f32)
    gains = jnp.dot(base_hot, gain_table.T, precision=highest)
    g0, g1 = gains[:, 0:1], gains[:, 1:2]
    re = total[:, 0]
    im = jnp.where(mine(mirrored)[:, None], -total[:, 1], total[:, 1])
    return jnp.stack([g0 * re - g1 * im, g0 * im + g1 * re], axis=1)[None]


def solution(mesh):
    return jax.shard_map(
        local,
        mesh=mesh,
        in_specs=(
            P("beam", "fft", None), P(), P("beam", None, None, None), P("beam"),
            P("beam", None, None), P("beam", None), P("beam", None),
            P("beam", None, None, None), P("beam", None), P(),
        ),
        out_specs=P("beam", "fft", None, None),
        check_vma=False,
    )
```

```python
import functools
import math

import jax
import jax.numpy as jnp
import numpy as np
from jax import lax
from jax.experimental import pallas as pl
from jax.experimental.pallas import tpu as pltpu
from jax.sharding import PartitionSpec as P

FT = 8
SG = 32
CAP = 8
LANES = 128
LAG = 12
TOGETHER = 4
OFF_LEAST, OFF_MOST = 2.0, 29.0
TURN_UNIT = 2.0**30
PROF_UNIT = 2.0**25
OFF_STEP = (OFF_MOST - OFF_LEAST) / 65535.0

kernel_width = 1.5
highest = lax.Precision.HIGHEST
f32 = jnp.float32
bf16 = jnp.bfloat16


def phase_table(rows, cols, period):
    angle = np.asarray(rows * cols % period) * (2.0 * math.pi / period)
    return jnp.asarray(np.stack([np.cos(angle), -np.sin(angle)]).astype(np.float32))


def turn_by(xr, xi, yr, yi):
    return xr * yr - xi * yi, xr * yi + xi * yr


def window_kernel(
    tix_ref, ti_ref, tj_ref, valid_ref, sub_ref,
    own_ref, oth_ref, v_coarse_ref, v_fine_ref, u_coarse_ref, u_fine_ref, ea_ref, eb_ref,
    *rest, ffts, quads, unroll,
):
    small_refs, rest = rest[:quads], rest[quads:]
    (out_ref, rs_ref, low_ref, flip_ref, prof_ref, off_ref, acc_ref,
     tcos_ref, tsin_ref, left_ref, a_ref, b_ref) = rest
    q = pl.program_id(0)
    my_beam = lax.axis_index("beam")
    my_fft = lax.axis_index("fft")
    my_core = lax.rem(my_fft, 2)
    fft_ids = (my_fft, my_fft + 1 - 2 * my_core)
    fine_v, fine_u = v_fine_ref.shape[1], u_fine_ref.shape[2]
    quad = lax.rem(my_beam // 2 + q, quads)
    half_side = own_ref.shape[2] // 2
    per_half = half_side // LANES
    per_tile = 2 * per_half
    first_v = FT * ffts
    subs = acc_ref.shape[0]
    prof_rows = prof_ref.shape[0]
    off_at = prof_rows + 4 * (subs // LANES)

    @pl.when(q == 0)
    def _():
        row = lax.broadcasted_iota(jnp.int32, (half_side, half_side), 0)
        col = lax.broadcasted_iota(jnp.int32, (half_side, half_side), 1)
        flip_ref[...] = (row + col == half_side - 1).astype(f32).astype(bf16)

        def some_rows(i, carry):
            for n in range(3):
                a = i * 3 + n
                cos, sin = turn_by(
                    v_coarse_ref[0, pl.ds(a, 1), :], v_coarse_ref[1, pl.ds(a, 1), :],
                    v_fine_ref[0], v_fine_ref[1])
                at = pl.ds(pl.multiple_of(a * fine_v, fine_v), fine_v)
                tcos_ref[at, :] = cos.astype(bf16)
                tsin_ref[at, :] = sin.astype(bf16)
                at = pl.ds(pl.multiple_of(a * fine_u, fine_u), fine_u)
                for h, f in enumerate(fft_ids):
                    cos, sin = turn_by(
                        u_coarse_ref[0, f, pl.ds(a, 1), :], u_coarse_ref[1, f, pl.ds(a, 1), :],
                        u_fine_ref[0, f], u_fine_ref[1, f])
                    left_ref[2 * h, at, :] = cos
                    left_ref[2 * h + 1, at, :] = sin
            return carry

        lax.fori_loop(0, v_coarse_ref.shape[1] // 3, some_rows, 0)

    lane = lax.broadcasted_iota(jnp.int32, (16, LANES), 1)
    for part in range(2):
        for half in range(2):
            a_rows, b_rows = ea_ref[part, 0], eb_ref[part, 0]
            for n in range(CAP // 2):
                here = lane // SG == n
                k = half * (CAP // 2) + n
                a_rows = jnp.where(here, ea_ref[part, ti_ref[q, k]], a_rows)
                b_rows = jnp.where(here[:8], eb_ref[part, tj_ref[q, k]], b_rows)
            a_ref[part, half] = a_rows
            b_ref[part, half] = b_rows

    for t in range(quads):
        @pl.when(q == t)
        def _():
            prof_ref[...] = small_refs[t][:prof_rows].astype(f32) * (1.0 / PROF_UNIT)
            for h in range(off_ref.shape[2] // LANES):
                code = small_refs[t][off_at + h * subs:off_at + (h + 1) * subs]
                pair = ((code & 65535).astype(f32), (code >> 16).astype(f32) + 32768.0)
                for n in range(2):
                    off_ref[n, :, h * LANES:(h + 1) * LANES] = pair[n] * OFF_STEP + OFF_LEAST

    def prof_row(at):
        return prof_ref[pl.ds(at, 1), :]

    low_prof = jnp.concatenate(
        [prof_ref[pl.ds(first_v + p, FT, stride=per_tile), :] for p in range(per_half)], axis=1)
    low_ref[...] = jnp.dot(
        low_prof, flip_ref[...].astype(f32), precision=highest, preferred_element_type=f32)

    def some_tiles(step, carry):
        even, odd, row_scales = [], [], []
        for n in range(TOGETHER):
            k = step * TOGETHER + n
            t, i, j = tix_ref[q, k], ti_ref[q, k], tj_ref[q, k]
            valid = valid_ref[q, k].astype(f32)
            scale_hi = jnp.concatenate(
                [prof_row(first_v + j * per_tile + p) for p in range(per_half, per_tile)], axis=1)
            scale_lo = low_ref[pl.ds(j, 1), :]
            lo = jnp.dot(
                jnp.concatenate([own_ref[t, :, :half_side], oth_ref[t, :, :half_side]], axis=0),
                flip_ref[...], preferred_element_type=f32) * scale_lo
            hi = jnp.concatenate(
                [own_ref[t, :, half_side:], oth_ref[t, :, half_side:]], axis=0).astype(f32) * scale_hi
            even.append((hi + lo).astype(bf16))
            odd.append((hi - lo).astype(bf16))
            for f in fft_ids:
                row_scales.append(prof_row(i * ffts + f) * valid)
        row_scale = jnp.concatenate(row_scales, axis=1)
        for c, (table, parts) in enumerate(((tcos_ref, even), (tsin_ref, odd))):
            got = lax.dot_general(
                table[...], jnp.concatenate(parts, axis=0), (((1,), (1,)), ((), ())),
                preferred_element_type=f32,
            ) * row_scale
            for n in range(TOGETHER):
                for h in range(2):
                    at = (2 * n + h) * LANES
                    rs_ref[h * 2 + c, step * TOGETHER + n] = got[:, at:at + LANES]
        return carry

    for step in range(CAP // TOGETHER):
        some_tiles(step, 0)

    samples = off_ref.shape[2]
    wide = lax.broadcasted_iota(jnp.int32, (2 * SG, LANES), 1)
    is_low = (wide // SG) == 1
    places = lax.broadcasted_iota(jnp.int32, (SG, samples), 0).astype(f32)
    factor = -math.log2(math.e) / kernel_width**2

    def cut_out(s):
        r0 = sub_ref[q, 0, s]
        code = sub_ref[q, 1, s]
        mirrored = code >= 2 * FT * half_side
        c0 = jnp.where(mirrored, code - 2 * FT * half_side, code)
        windows = jnp.concatenate([
            jnp.concatenate([rs_ref[j, k, pl.ds(c0, SG), :].astype(bf16) for j in range(4)], axis=1)
            for k in range(CAP)
        ], axis=0)
        lr0, li0, lr1, li1 = (left_ref[n, pl.ds(r0, SG), :].astype(bf16) for n in range(4))
        left = jnp.concatenate([
            jnp.concatenate([lr0, -li0, lr1, -li1], axis=1),
            jnp.concatenate([li0, lr0, li1, lr1], axis=1),
        ], axis=0)
        out = lax.dot_general(left, windows, (((1,), (1,)), ((), ())), preferred_element_type=f32)
        r8, c8 = lax.rem(r0, 8), lax.rem(c0, 8)
        ar, ai = (
            jnp.concatenate([a_ref[part, half, pl.ds(r8, 8), :] for half in range(2)], axis=1)
            for part in range(2))
        br, bi = (
            jnp.concatenate([b_ref[part, half, pl.ds(c8, 1), :] for half in range(2)], axis=1)
            for part in range(2))
        br, bi = turn_by(br, bi, sub_ref[q, 2, s].astype(f32) * (1.0 / TURN_UNIT), sub_ref[q, 3, s].astype(f32) * (1.0 / TURN_UNIT))
        fr, fi = turn_by(ar, ai, br, bi)
        re_parts, im_parts = [], []
        for a in range(SG // 8):
            re, im = turn_by(out[a * 8:(a + 1) * 8], out[SG + a * 8:SG + (a + 1) * 8], fr, fi)
            re_parts.append(re)
            im_parts.append(im)
        full = jnp.concatenate(re_parts + im_parts, axis=0)
        half = full[:, :LANES] + full[:, LANES:]
        half = half + pltpu.roll(half, 2 * SG, 1)
        half = half + pltpu.roll(half, SG, 1)
        low = half - half.astype(bf16).astype(f32)
        return jnp.where(is_low, low, half).astype(bf16)

    def degrid(s, cut):
        mirrored = sub_ref[q, 1, s] >= 2 * FT * half_side
        base = jnp.where(mirrored, SG - 1.0, 0.0)
        way = jnp.where(mirrored, -1.0, 1.0)
        at = places * way + base
        tu = at - off_ref[0, pl.ds(s, 1), :]
        tv = at - off_ref[1, pl.ds(s, 1), :]
        wu = jnp.exp2(tu * tu * factor)
        wv = jnp.exp2(tv * tv * factor)
        wv_high = wv.astype(bf16)
        wv_low = (wv - wv_high.astype(f32)).astype(bf16)
        right = jnp.concatenate([wv_high, wv_high, wv_low], axis=0)
        inner = jnp.dot(cut[:, :3 * SG], right, preferred_element_type=f32)
        re = jnp.sum(inner[:SG] * wu, axis=0, keepdims=True)
        im = jnp.sum(inner[SG:] * wu, axis=0, keepdims=True)
        return jnp.concatenate([re, im], axis=1)

    def some_subs(i, carry):
        cuts, rows = [], []
        for u in range(unroll + LAG):
            if u < unroll:
                cuts.append(cut_out(i * unroll + u))
            if u >= LAG:
                rows.append(degrid(i * unroll + u - LAG, cuts[u - LAG]))
        acc_ref[pl.ds(pl.multiple_of(i * unroll, unroll), unroll), :] = jnp.concatenate(rows, axis=0)
        return carry

    lax.fori_loop(0, subs // unroll, some_subs, 0)
    sub_dev = subs // ffts
    for f in range(ffts):
        out_ref[quad, f % 2, f // 2] = acc_ref[f * sub_dev:(f + 1) * sub_dev].astype(out_ref.dtype)


def local(
    sky_model, footprint, profile, chan_block, sub_strip, sub_row, sub_col,
    offsets, sub_base, gain_table,
):
    axes = ("beam", "fft")
    beams = lax.axis_size("beam")
    ffts = lax.axis_size("fft")
    my_fft = lax.axis_index("fft")
    quads = beams // 2
    pairs = ffts // 2
    tiles_dev, tile_rows, tile_side = sky_model.shape
    image_side = FT * tile_side
    half_side = image_side // 2
    subs = sub_row.shape[1]
    sub_dev = subs // ffts
    samples = offsets.shape[3]
    strip_cols = image_side // ffts

    def turn(step):
        out = []
        for b in range(beams):
            for f in range(ffts):
                target = (2 * ((b // 2 - step) % quads) + f % 2) * ffts + 2 * (f // 2) + b % 2
                out.append((b * ffts + f, target))
        return out

    oth_sky = lax.ppermute(sky_model, "fft", [(f, f ^ 1) for f in range(ffts)])

    chosen = lax.dynamic_index_in_dim(profile[0], chan_block[0], 0, keepdims=False)
    col_at = sub_strip[0, :, 0] * strip_cols + sub_col[0]
    mirrored = col_at >= half_side
    r0_mine = jnp.where(mirrored, (image_side - (SG - 1) - sub_row[0]) % image_side, sub_row[0])
    c0_mine = jnp.where(mirrored, image_side - (SG - 1) - col_at, col_at)
    middle = 2 * image_side
    angle = ((tile_side - 1) * c0_mine % middle).astype(f32) * (2.0 * math.pi / middle)
    code_mine = jnp.where(mirrored, c0_mine + image_side, c0_mine)
    per_sub = [r0_mine, code_mine] + [(x * TURN_UNIT).astype(jnp.int32) for x in (jnp.cos(angle), -jnp.sin(angle))]
    prof_int = (chosen * PROF_UNIT).astype(jnp.int32)
    prof_u = jnp.pad(prof_int[0].reshape(FT * ffts, tile_rows), ((0, 0), (0, LANES - tile_rows)))
    off_code = jnp.round((offsets[0] - OFF_LEAST) * (1.0 / OFF_STEP)).astype(jnp.int32)
    off_code = off_code[:, 0] + (off_code[:, 1] - 32768) * 65536
    small = jnp.concatenate(
        [prof_u, prof_int[1].reshape(-1, LANES)] + [x.reshape(-1, LANES) for x in per_sub]
        + [off_code[:, at:at + LANES] for at in range(0, samples, LANES)])
    smalls = [lax.ppermute(small, axes, turn(t)) for t in range(quads)]
    prof_rows = FT * ffts + image_side // LANES
    sub_rows = subs // LANES
    sub_parts = jnp.stack([x[prof_rows:prof_rows + 4 * sub_rows] for x in smalls]).reshape(quads, 4, subs)

    my_beam = lax.axis_index("beam")
    beam_ids = 2 * ((my_beam // 2 + jnp.arange(quads, dtype=jnp.int32)) % quads) + my_fft % 2
    pick_beam = beam_ids[:, None, None] == jnp.arange(beams, dtype=jnp.int32)[None, :, None]
    lists = jnp.sum(jnp.where(pick_beam, footprint[None], 0), axis=1)
    hits = lists // tiles_dev == my_beam
    entry = jnp.arange(FT * FT, dtype=jnp.int32)
    earlier = entry[None, :] < entry[:, None]
    order = jnp.sum(jnp.where(hits[:, None, :] & earlier[None], 1, 0), axis=2)
    slots = hits[:, None, :] & (order[:, None, :] == jnp.arange(CAP, dtype=jnp.int32)[None, :, None])
    in_slot = lambda values: jnp.sum(jnp.where(slots, values, 0), axis=2)
    tix = in_slot((lists % tiles_dev)[:, None, :])
    tile_i, tile_j = in_slot(entry // FT), in_slot(entry % FT)
    valid = in_slot(1)

    side_half = tile_side // 2
    coarse, fine_v, fine_u = 129, image_side // 256, SG
    v_col = 2 * np.arange(side_half) + 1
    v_coarse = phase_table(fine_v * np.arange(coarse)[:, None], v_col, middle)
    v_fine = phase_table(np.arange(fine_v)[:, None], v_col, middle)
    u_col = np.arange(ffts)[:, None, None] * tile_rows + np.arange(LANES)
    u_coarse = phase_table(fine_u * np.arange(coarse)[:, None], u_col, image_side)
    u_fine = phase_table(np.arange(fine_u)[:, None], u_col, image_side)
    lane_e = np.arange(LANES) % SG
    eights = np.arange(FT)[:, None, None]
    ea = phase_table(eights * np.arange(16)[:, None], np.ones(LANES, np.int64), FT)
    eb = phase_table(
        middle // FT * eights * (np.arange(8)[:, None] + lane_e) + (tile_side - 1) * lane_e, 1, middle)
    v_rows, u_rows = coarse * fine_v, coarse * fine_u
    if tile_rows < LANES:
        pad_rows = ((0, 0), (0, LANES - tile_rows), (0, 0))
        sky_model, oth_sky = jnp.pad(sky_model, pad_rows), jnp.pad(oth_sky, pad_rows)

    whole = lambda a: pl.BlockSpec(a.shape, lambda q, *_: (0,) * a.ndim, pipeline_mode=pl.Buffered(1))
    fixed = [sky_model, oth_sky, v_coarse, v_fine, u_coarse, u_fine, ea, eb, *smalls]
    out_shape = (quads, 2, pairs, sub_dev, 2 * samples)
    partial = pl.pallas_call(
        functools.partial(window_kernel, ffts=ffts, quads=quads, unroll=64),
        out_shape=jax.ShapeDtypeStruct(out_shape, bf16),
        grid_spec=pltpu.PrefetchScalarGridSpec(
            num_scalar_prefetch=5, grid=(quads,),
            in_specs=[whole(x) for x in fixed],
            out_specs=pl.BlockSpec(out_shape, lambda q, *_: (0,) * len(out_shape)),
            scratch_shapes=[
                pltpu.VMEM((4, CAP, v_rows, LANES), f32),
                pltpu.VMEM((FT, side_half), f32),
                pltpu.VMEM((side_half, side_half), bf16),
                pltpu.VMEM((prof_rows, LANES), f32),
                pltpu.VMEM((2, subs, samples), f32),
                pltpu.VMEM((subs, 2 * samples), f32),
                pltpu.VMEM((v_rows, side_half), bf16),
                pltpu.VMEM((v_rows, side_half), bf16),
                pltpu.VMEM((4, u_rows, LANES), f32),
                pltpu.VMEM((2, 2, 16, LANES), f32),
                pltpu.VMEM((2, 2, 8, LANES), f32),
            ],
        ),
        compiler_params=pltpu.CompilerParams(vmem_limit_bytes=63 << 20),
        name="windows",
    )(tix, tile_i, tile_j, valid, sub_parts, *fixed)

    groups = [[b * ffts + 2 * x + c for b in range(beams) for x in range(pairs)] for c in range(2)]
    parts = partial.reshape(beams * pairs, sub_dev, 2 * samples)
    came = lax.all_to_all(parts, axes, 0, 0, tiled=True, axis_index_groups=groups)
    total = jnp.sum(came.astype(f32), axis=0)
    total = lax.ppermute(total, axes, turn(0)) * (1.0 / image_side)
    total = total.reshape(sub_dev, 2, samples)

    mine = lambda a: lax.dynamic_slice_in_dim(a, my_fft * sub_dev, sub_dev, 0)
    base_hot = (mine(sub_base[0])[:, None] == jnp.arange(gain_table.shape[1], dtype=jnp.int32)[None, :]).astype(f32)
    gains = jnp.dot(base_hot, gain_table.T, precision=highest)
    g0, g1 = gains[:, 0:1], gains[:, 1:2]
    re = total[:, 0]
    im = jnp.where(mine(mirrored)[:, None], -total[:, 1], total[:, 1])
    return jnp.stack([g0 * re - g1 * im, g0 * im + g1 * re], axis=1)[None]


def solution(mesh):
    return jax.shard_map(
        local,
        mesh=mesh,
        in_specs=(
            P("beam", "fft", None), P(), P("beam", None, None, None), P("beam"),
            P("beam", None, None), P("beam", None), P("beam", None),
            P("beam", None, None, None), P("beam", None), P(),
        ),
        out_specs=P("beam", "fft", None, None),
        check_vma=False,
    )
```
